128 devices in a mesh: win: 4 (over z_lo, core), chan: 32 (over y, z_hi, x).
Axes of the slice: x: 4, y: 4, z: 4 (z_hi: 2, z_lo: 2; z = z_hi * 2 + z_lo), core: 2. Of those that a mesh axis runs over, the one named last changes fastest.
Arguments:
- traces: bfloat16 [32, 1024, 7680], P('win', 'chan'), may hold values from -6 to 6
- filter_taps: bfloat16 [32], replicated, may hold values from 0.019897461 to 0.14941406
- good_channels: int32 [1024], P('chan'), may hold values 0 or 1
- source_index: int32 [256], replicated, may hold values from 0 to 1023, as said below
Outputs:
- correlations: float32 [256, 1024, 2048], P('win', 'chan')
The draws below stay inside these ranges and needn't reach their ends.
Inputs may be any that keep to these rules, and one draw needn't show every extreme that they name: `source_index`: 256 distinct channel numbers; channels 0 and 1023 are among them; how many fall in one device's block varies.
All inputs are finite; a program needn't handle non-finite values. No bound on the sum of `good_channels` on one device may be relied on, other than what follows from the above.
Results may differ from the reference program's by a relative error of at most 0.0071.
Values may be sent and summed in bfloat16 or wider, within the bound.
A program may use at most 192 MiB of HBM per device.

```python
import math
import jax
import jax.numpy as jnp
from jax import lax

L = 7680
F = 512
LAGS = 2048
S = 256
HALO = 16
SMOOTH = 64
K0 = 31
CH = 1024
WINDOWS = 32


def draw_source_index(key, part):
    key_first, key_second = jax.random.split(jax.random.fold_in(key, 7))
    middle = jax.random.permutation(key_first, CH - 2)[:S - 2].astype(jnp.int32) + 1
    chosen = jnp.concatenate([jnp.array([0, CH - 1], jnp.int32), middle])
    shuffle = jax.random.permutation(key_second, S)
    return chosen[shuffle].astype(jnp.int32)


def touch_ends(result, own_key, least, largest):
    place = [jax.random.randint(jax.random.fold_in(own_key, axis), (), 0, length) for axis, length in enumerate(result.shape)]
    main_axis = result.shape.index(max(result.shape))
    beside = place[:main_axis] + [(place[main_axis] + 1) % result.shape[main_axis]] + place[main_axis + 1:]
    return result.at[tuple(place)].set(least).at[tuple(beside)].set(largest)


def shard_levels(rng, extent, cuts, low, largest):
    loudness, own = 1.0, jax.random.fold_in(rng, 6)
    for axis_at, shards_of in cuts:
        heights = jnp.exp(jax.random.uniform(jax.random.fold_in(own, axis_at), (shards_of,), jnp.float32, low / len(cuts), largest / len(cuts)))
        loudness = loudness * jnp.repeat(heights, extent[axis_at] // shards_of).reshape([-1 if axis == axis_at else 1 for axis in range(len(extent))])
    return loudness


def noise(rng, dims, scale, most, pieces=(), kind=jnp.bfloat16):
    factor_of = shard_levels(rng, dims, pieces, -0.22, 0.18) if pieces else 1.0
    values = jax.random.normal(rng, dims, jnp.float32) * scale * factor_of
    return jnp.minimum(jnp.maximum(values, -most), most).astype(kind)


def setup_inputs(seed: int = 0) -> dict:
    keys = jax.random.split(jax.random.key(seed), 5)
    return {
        "traces": noise(keys[0], (WINDOWS, CH, L), 1.0, 6.0, ((0, 4), (1, 32))),
        "filter_taps": jnp.clip(jnp.exp(jax.random.uniform(keys[1], (2 * HALO,), jnp.float32, math.log(0.019897461), math.log(0.14941406))), 0.019897461, 0.14941406).astype(jnp.bfloat16),
        "good_channels": touch_ends((jax.random.randint(keys[2], (CH,), 0, 16) < 15).astype(jnp.int32), jax.random.fold_in(keys[2], 1), 0, 1),
        "source_index": draw_source_index(jax.random.fold_in(keys[4], 71), 0),
    }


def forward_table():
    times_idx = jnp.arange(L, dtype=jnp.int32)
    band_bins = K0 + jnp.arange(F, dtype=jnp.int32)
    phase_index = times_idx[:, None] * band_bins[None, :] % L
    angles = phase_index.astype(jnp.float32) * (2.0 * math.pi / L)
    return jnp.concatenate([jnp.cos(angles), -jnp.sin(angles)], axis=1).astype(jnp.bfloat16)

def inverse_table():
    lag_values = jnp.arange(LAGS, dtype=jnp.int32) - LAGS // 2
    band_bins = K0 + jnp.arange(F, dtype=jnp.int32)
    phase_index = jnp.mod(band_bins[:, None] * lag_values[None, :], L)
    angles = phase_index.astype(jnp.float32) * (2.0 * math.pi / L)
    return jnp.concatenate([jnp.cos(angles), -jnp.sin(angles)], axis=0).astype(jnp.bfloat16)

def smoothing():
    positions = jnp.arange(F, dtype=jnp.int32)
    near = (jnp.abs(positions[:, None] - positions[None, :]) <= SMOOTH).astype(jnp.float32)
    return near / lax.optimization_barrier(jnp.sum(near, axis=0, keepdims=True))

def whiten(spectrum):
    real_part = spectrum[..., :F]
    imag_part = spectrum[..., F:]
    magnitude = jnp.sqrt(real_part * real_part + imag_part * imag_part)
    flat = magnitude.reshape(-1, F)
    amplitude = jnp.dot(flat, smoothing(), precision=lax.Precision.HIGHEST).reshape(magnitude.shape)
    divisor = jnp.concatenate([amplitude, amplitude], axis=-1) + 1e-06
    return (spectrum / divisor).astype(jnp.bfloat16)

def reference(traces, filter_taps, good_channels, source_index):
    kernel = jnp.concatenate([-filter_taps[:HALO].astype(jnp.float32), jnp.ones((1,), jnp.float32), -filter_taps[HALO:].astype(jnp.float32)])
    masked = traces * good_channels.astype(jnp.bfloat16)[None, :, None]
    keep = good_channels.astype(jnp.float32)[:, None]
    table = forward_table()

    def one_window(window):
        padded = jnp.pad(window, ((HALO, HALO), (0, 0))).astype(jnp.float32)
        total = jnp.zeros((CH, L), jnp.float32)
        for position in range(2 * HALO + 1):
            total = total + kernel[position] * padded[position:position + CH]
        filtered = (total * keep).astype(jnp.bfloat16)
        spectrum = jnp.dot(filtered, table, preferred_element_type=jnp.float32)
        return whiten(spectrum)
    whitened = lax.map(one_window, masked)
    wide = whitened.astype(jnp.float32)
    wide_real = wide[..., :F]
    wide_imag = wide[..., F:]
    picked = jnp.transpose(jnp.take(whitened, source_index.astype(jnp.int32), axis=1), (1, 0, 2))
    inverse = inverse_table()
    scaling = 1.0 / math.sqrt(F * WINDOWS)
    high = lax.Precision.HIGHEST

    def one_source(spectra):
        source = spectra.astype(jnp.float32)
        src_real = source[:, :F]
        src_imag = source[:, F:]
        real_sum = jnp.einsum('wf,wcf->cf', src_real, wide_real, precision=high) + jnp.einsum('wf,wcf->cf', src_imag, wide_imag, precision=high)
        imag_sum = jnp.einsum('wf,wcf->cf', src_real, wide_imag, precision=high) - jnp.einsum('wf,wcf->cf', src_imag, wide_real, precision=high)
        stacked = jnp.concatenate([real_sum, imag_sum], axis=-1).astype(jnp.bfloat16)
        return jnp.dot(stacked, inverse, preferred_element_type=jnp.float32) * scaling
    return lax.map(one_source, picked)
```

```python
import math

import jax
import jax.numpy as jnp
from jax import lax
from jax.sharding import PartitionSpec as P

L = 7680
F = 512
LAGS = 2048
HALO = 16
SMOOTH = 64
K0 = 31


def turn(bins, steps):
    phase = jnp.mod(bins * steps, L).astype(jnp.float32) * (2.0 * math.pi / L)
    return jnp.cos(phase), jnp.sin(phase)


def forward_table():
    bins = K0 + jnp.arange(F, dtype=jnp.int32)
    step = 64
    ca, sa = turn(bins[None, :], step * jnp.arange(L // step, dtype=jnp.int32)[:, None])
    cb, sb = turn(bins[None, :], jnp.arange(step, dtype=jnp.int32)[:, None])
    ca, sa, cb, sb = lax.optimization_barrier((ca, sa, cb, sb))
    cosine = ca[:, None] * cb[None] - sa[:, None] * sb[None]
    sine = sa[:, None] * cb[None] + ca[:, None] * sb[None]
    return (
        cosine.reshape(L, F).astype(jnp.bfloat16),
        (-sine).reshape(L, F).astype(jnp.bfloat16),
    )


def inverse_table():
    bins = (K0 + jnp.arange(F, dtype=jnp.int32))[:, None]
    step = 128
    ca, sa = turn(bins, step * jnp.arange(LAGS // step, dtype=jnp.int32)[None, :] - LAGS // 2)
    cb, sb = turn(bins, jnp.arange(step, dtype=jnp.int32)[None, :])
    ca, sa, cb, sb = lax.optimization_barrier((ca, sa, cb, sb))
    cosine = ca[:, :, None] * cb[:, None] - sa[:, :, None] * sb[:, None]
    sine = sa[:, :, None] * cb[:, None] + ca[:, :, None] * sb[:, None]
    return (
        cosine.reshape(F, LAGS).astype(jnp.bfloat16),
        (-sine).reshape(F, LAGS).astype(jnp.bfloat16),
    )


def smoothing():
    positions = jnp.arange(F, dtype=jnp.int32)
    near = (jnp.abs(positions[:, None] - positions[None, :]) <= SMOOTH).astype(jnp.float32)
    return near / jnp.sum(near, axis=0, keepdims=True)


def make_band(filter_taps, channel_count):
    kernel = jnp.concatenate(
        [
            -filter_taps[:HALO].astype(jnp.float32),
            jnp.ones((1,), jnp.float32),
            -filter_taps[HALO:].astype(jnp.float32),
        ]
    )
    row_ids = jnp.arange(channel_count, dtype=jnp.int32)[:, None]
    columns = jnp.arange(channel_count + 2 * HALO, dtype=jnp.int32)[None, :]
    offset = columns - row_ids
    choose = offset[:, :, None] == jnp.arange(2 * HALO + 1, dtype=jnp.int32)[None, None, :]
    return jnp.sum(jnp.where(choose, kernel[None, None, :], 0.0), axis=2)


def with_halo(cells, axis, dim, width):
    count = lax.axis_size(axis)
    ends = count - 1
    head = lax.slice_in_dim(cells, 0, width, axis=dim)
    tail = lax.slice_in_dim(cells, cells.shape[dim] - width, cells.shape[dim], axis=dim)
    before = lax.ppermute(tail, axis, [(i, (i + 1) % count) for i in range(ends)])
    after = lax.ppermute(head, axis, [((i + 1) % count, i) for i in range(ends)])
    return jnp.concatenate([before, cells, after], axis=dim)


def per_device(traces, filter_taps, good_channels, source_index):
    windows, channels, length = traces.shape
    groups, blocks = lax.axis_size("win"), lax.axis_size("chan")
    sources = source_index.shape[0]
    bins = F // blocks
    everyone = channels * blocks
    good = good_channels.astype(jnp.float32)[None, :, None]

    rows = traces.reshape(windows * channels, length)
    cosine, sine = forward_table()
    dot = lambda a, b: jnp.dot(a, b, preferred_element_type=jnp.float32)
    spectrum = jnp.stack([dot(rows, cosine), dot(rows, sine)], axis=1)
    spectrum = spectrum.reshape(windows, channels, 2 * F) * good
    padded = with_halo(spectrum, "chan", 1, HALO)
    band = make_band(filter_taps, channels)
    filtered = jnp.einsum("cd,wdf->wcf", band, padded, precision=lax.Precision.HIGHEST) * good

    real, imag = filtered[..., :F], filtered[..., F:]
    magnitude = jnp.sqrt(real * real + imag * imag).reshape(-1, F)
    amplitude = jnp.dot(magnitude, smoothing(), precision=lax.Precision.HIGHEST)
    divisor = amplitude.reshape(real.shape) + 1e-06
    whitened = jnp.stack([real / divisor, imag / divisor], axis=2).astype(jnp.bfloat16)

    split = whitened.reshape(windows, channels, 2, blocks, bins)
    split = jnp.transpose(split, (3, 4, 2, 0, 1)).reshape(blocks, bins * 2, windows * channels)
    mixed = lax.all_to_all(split, "chan", 0, 0, tiled=True)
    mixed = mixed.reshape(blocks, bins * 2 * windows, channels)
    mixed = jnp.transpose(mixed, (1, 0, 2)).reshape(bins * 2 * windows, everyone)
    ids = jnp.arange(everyone, dtype=jnp.int32)
    selector = (ids[:, None] == source_index[None, :]).astype(jnp.bfloat16)
    picked = dot(mixed, selector).astype(jnp.bfloat16)
    share = sources // groups
    picked = picked.reshape(bins * 2 * windows, groups, share)
    picked = jnp.transpose(picked, (1, 0, 2))
    picked = lax.all_to_all(picked, "win", 0, 0, tiled=True)
    picked = picked.reshape(groups, bins, 2, windows, share)
    picked = jnp.transpose(picked, (1, 2, 0, 3, 4)).reshape(bins, groups * windows, 2 * share)
    gathered = lax.all_gather(picked, "chan", axis=0, tiled=True)
    gathered = gathered.reshape(F, 2 * groups * windows, share)

    own = lax.all_gather(whitened, "win", axis=0, tiled=True)
    own = jnp.transpose(own, (3, 2, 0, 1))
    own_real, own_imag = own[:, 0], own[:, 1]
    left = jnp.concatenate([own_real, own_imag], axis=1)
    right = jnp.concatenate([own_imag, -own_real], axis=1)
    both = jnp.concatenate([left, right], axis=2)
    stacked = jnp.einsum("fks,fkc->fsc", gathered, both, preferred_element_type=jnp.float32)
    stacked = stacked.astype(jnp.bfloat16).reshape(F, share, 2, channels)
    stacked = jnp.transpose(stacked, (1, 3, 2, 0)).reshape(share * channels, 2, F)
    scaling = 1.0 / math.sqrt(F * windows * groups)
    cosine, sine = inverse_table()
    lagged = (dot(stacked[:, 0], cosine) + dot(stacked[:, 1], sine)) * scaling
    return lagged.reshape(share, channels, LAGS)


def solution(mesh):
    placed = (P("win", "chan", None), P(), P("chan"), P())
    return jax.shard_map(
        per_device, mesh=mesh, in_specs=placed, out_specs=P("win", "chan", None), check_vma=False
    )
```

```python
import functools
import math

import jax
import jax.numpy as jnp
from jax import lax
from jax.experimental import pallas as pl
from jax.experimental.pallas import tpu as pltpu
from jax.sharding import PartitionSpec as P

L = 7680
F = 512
LAGS = 2048
HALO = 16
SMOOTH = 64
K0 = 31

WIN = 4
BLK = 32
NX = 4
NZ = 2
NY = 4
W = 8
C = 32
S = 64
BINS = F // BLK
QUADS = F // 4
PACK = 4
DEEP = 2 * W * WIN
MESH = pl.DeviceIdType.MESH
f32, bf16, i32 = jnp.float32, jnp.bfloat16, jnp.int32


def iota(shape, dim):
    return lax.broadcasted_iota(i32, shape, dim)


def mxu(a, b):
    return jnp.dot(a, b, preferred_element_type=f32)


def loop(start, stop, body):
    def step(i, carry):
        body(i)
        return carry

    lax.fori_loop(start, stop, step, 0)


def thirds(x):
    high = x.astype(bf16)
    rest = x - high.astype(f32)
    middle = rest.astype(bf16)
    low = (rest - middle.astype(f32)).astype(bf16)
    return high, middle, low


def chan_copy(src, dst, send, recv, peer):
    return pltpu.make_async_remote_copy(
        src_ref=src, dst_ref=dst, send_sem=send, recv_sem=recv,
        device_id=(lax.axis_index("win"), peer), device_id_type=MESH,
    )


def win_copy(src, dst, send, recv, peer):
    return pltpu.make_async_remote_copy(
        src_ref=src, dst_ref=dst, send_sem=send, recv_sem=recv,
        device_id=(peer, lax.axis_index("chan")), device_id_type=MESH,
    )


def middle(
    spec, keep, band, near, share, sources, order, quads, own,
    low, high, white, outgoing, mixed, chosen, regroup,
    halo_send, halo_recv, all_send, all_recv, own_send, own_recv, win_send, win_recv,
):
    me = lax.axis_index("chan")
    group = lax.axis_index("win")

    barrier = pltpu.get_barrier_semaphore()

    def greet_chan(k):
        pl.semaphore_signal(barrier, inc=1, device_id=(group, lax.rem(me + k, BLK)), device_id_type=MESH)

    def greet_win(k):
        pl.semaphore_signal(barrier, inc=1, device_id=(lax.rem(group + k, WIN), me), device_id_type=MESH)

    loop(1, BLK, greet_chan)
    loop(1, WIN, greet_win)
    pl.semaphore_wait(barrier, BLK + WIN - 2)

    right, left = lax.rem(me + 1, BLK), lax.rem(me + BLK - 1, BLK)

    def to_right(w):
        return chan_copy(spec.at[w, pl.ds(C - HALO, HALO)], low.at[w], halo_send.at[0, w], halo_recv.at[0, w], right)

    def to_left(w):
        return chan_copy(spec.at[w, pl.ds(0, HALO)], high.at[w], halo_send.at[1, w], halo_recv.at[1, w], left)

    def send_halo(w):
        @pl.when(me < BLK - 1)
        def _():
            to_right(w).start()

        @pl.when(me > 0)
        def _():
            to_left(w).start()


    loop(0, W, send_halo)

    @pl.when(me == 0)
    def _():
        low[...] = jnp.zeros_like(low)

    @pl.when(me == BLK - 1)
    def _():
        high[...] = jnp.zeros_like(high)

    def window(w):
        @pl.when(me > 0)
        def _():
            to_right(w).wait_recv()

        @pl.when(me < BLK - 1)
        def _():
            to_left(w).wait_recv()

        padded = jnp.concatenate([low[w], spec[w], high[w]], axis=0)
        taps = band[...]
        parts = thirds(padded)
        filtered = (mxu(taps, parts[0]) + mxu(taps, parts[1]) + mxu(taps, parts[2])) * keep[...]
        real, imag = filtered[:, :F], filtered[:, F:]
        magnitude = jnp.sqrt(real * real + imag * imag)
        sums = mxu(jnp.concatenate(thirds(magnitude), axis=0), near[...])
        amplitude = (sums[:C] + sums[C : 2 * C] + sums[2 * C :]) * share[...]
        divisor = amplitude + 1e-06
        out = jnp.concatenate([real / divisor, imag / divisor], axis=1)
        white[w] = out
        own[group, pl.ds(pl.multiple_of(w * C, C), C), :] = out.astype(bf16)

    loop(0, W, window)

    tiles = F // 128
    per_tile = 128 // BINS
    lane = iota((C, 128), 1) // BINS

    def regroup_tile(t):
        part, tile = t // tiles, lax.rem(t, tiles)
        columns = pl.ds(pl.multiple_of(t * 128, 128), 128)
        values = [white[w, :, columns] for w in range(W)]
        for m in range(per_tile):
            total = jnp.zeros((C, 128), f32)
            for w in range(W):
                shift = (w - m) * BINS % 128
                moved = pltpu.roll(values[w], shift, 1) if shift else values[w]
                total = jnp.where(lane == w, moved, total)
            outgoing[tile * per_tile + m, :, pl.ds(pl.multiple_of(part * 128, 128), 128)] = total.astype(bf16)

    loop(0, 2 * tiles, regroup_tile)

    def exchange(k):
        peer = lax.rem(me + k, BLK)
        return chan_copy(outgoing.at[peer], mixed.at[me], all_send.at[k], all_recv.at[k], peer)

    def exchange_start(k):
        exchange(k).start()

    loop(1, BLK, exchange_start)

    def share_own(k):
        peer = lax.rem(group + k, WIN)
        return win_copy(own.at[group], own.at[group], own_send.at[k], own_recv.at[k], peer)

    def own_start(k):
        share_own(k).start()

    loop(1, WIN, own_start)
    mixed[me] = outgoing[me]

    def exchange_wait(k):
        exchange(k).wait_recv()

    loop(1, BLK, exchange_wait)
    wanted = jnp.where(iota((WIN * S, BLK * C), 1) == sources[...], 1.0, 0.0).astype(bf16)
    picked = mxu(wanted, mixed[...].reshape(BLK * C, 2 * W * BINS)).astype(bf16)
    chosen[...] = picked.reshape(WIN, S, 2 * W * BINS)

    def trade(k):
        peer = lax.rem(group + k, WIN)
        return win_copy(chosen.at[peer], regroup.at[group], win_send.at[k], win_recv.at[k], peer)

    def trade_start(k):
        trade(k).start()

    loop(1, WIN, trade_start)
    regroup[group] = chosen[group]

    def trade_wait(k):
        trade(k).wait_recv()

    loop(1, WIN, trade_wait)
    arranged = mxu(regroup[0], order[0])
    for g in range(1, WIN):
        arranged += mxu(regroup[g], order[g])
    for q in range(BINS // PACK):
        quads[q] = arranged[:, q * 256 : (q + 1) * 256].astype(bf16)

    def finish_win(k):
        trade(k).wait_send()
        share_own(k).wait()

    def finish_chan(k):
        exchange(k).wait_send()

    def finish_halo(w):
        @pl.when(me < BLK - 1)
        def _():
            to_right(w).wait_send()

        @pl.when(me > 0)
        def _():
            to_left(w).wait_send()


    loop(1, WIN, finish_win)
    loop(1, BLK, finish_chan)
    loop(0, W, finish_halo)


def gather_cross(
    quads, own, far_cos, far_sin, near_cos, near_sin, stacked, inverse,
    held, turned, wide, crossed, send, recv,
):
    me = lax.axis_index("chan")
    group = lax.axis_index("win")
    y, z, x = me // (NZ * NX), lax.rem(me // NX, NZ), lax.rem(me, NX)

    def at(yy, zz, xx):
        return (lax.rem(yy + NY, NY) * NZ + lax.rem(zz, NZ)) * NX + lax.rem(xx + NX, NX)

    y_up, y_down, x_up, x_down, z_over = at(y + 1, z, x), at(y - 1, z, x), at(y, z, x + 1), at(y, z, x - 1), at(y, z + 1, x)

    barrier = pltpu.get_barrier_semaphore()
    for peer in (y_up, y_down, x_up, x_down, z_over):
        pl.semaphore_signal(barrier, inc=1, device_id=(group, peer), device_id_type=MESH)
    pl.semaphore_wait(barrier, 5)

    first = ((y_up, y_down), (x_up, x_down))
    last = ((x_up, x_down), (y_up, y_down))
    per_half = BINS // PACK // 2

    def piece(block, half):
        return held.at[block, pl.ds(half * per_half, per_half)]

    def hop(block, half, slot, peer, src=None):
        src = piece(block, half) if src is None else src
        return chan_copy(src, piece(block, half), send.at[block, half, slot], recv.at[block, half], peer)

    def own_piece(half):
        return quads.at[pl.ds(half * per_half, per_half)]

    def arrived(block, half):
        hop(block, half, 0, z_over).wait_recv()

    def cross(block, half):
        for j in range(per_half):
            quad = block * (2 * per_half) + half * per_half + j
            rows = pl.ds(pl.multiple_of(quad * S, S), S)
            result = mxu(held[block, half * per_half + j], wide[quad])
            crossed[0, rows, :] = result[:, :128]
            crossed[1, rows, :] = result[:, 128:]

    def spread_last(block, half, src=None):
        hop(block, half, 3, last[half][0], src).start()
        hop(block, half, 4, last[half][1], src).start()

    def spread(block, half, src=None):
        hop(block, half, 1, first[half][0], src).start()
        hop(block, half, 2, first[half][1], src).start()
        spread_last(block, half, src)

    def walk(i):
        k = i // NZ
        k = jnp.where(k > 1, 5 - k, k)
        return lax.rem(y + k, NY), lax.rem(x + k, NX), lax.rem(i, NZ)

    for half in (0, 1):
        hop(me, half, 0, z_over, own_piece(half)).start()
    for half in (0, 1):
        spread(me, half, own_piece(half))
    for q in range(2 * per_half):
        held[me, q] = quads[q]

    tiles = F // 128

    def turn_tile(t):
        part_tile, eight = t // 8, lax.rem(t, 8)
        part, tile = part_tile // tiles, lax.rem(part_tile, tiles)
        block = own[pl.ds(pl.multiple_of(eight * 128, 128), 128), pl.ds(pl.multiple_of(part_tile * 128, 128), 128)]
        turned[pl.ds(tile * 128 * 16 + part * 8 + eight, 128, stride=16), :] = block.astype(f32).T

    loop(0, 2 * tiles * 8, turn_tile)

    for half in (0, 1):
        arrived(z_over, half)
        spread(z_over, half)

    lane = iota((8, 128), 1) // 32
    blank = jnp.zeros((16, 128), bf16)

    def widen(quad):
        for b in range(PACK):
            base = pl.multiple_of((quad * PACK + b) * 16, 16)
            real, imag = turned[pl.ds(base, 8), :], turned[pl.ds(base + 8, 8), :]
            reals = [real] + [pltpu.roll(real, 32 * k, 1) for k in range(1, 4)]
            imags = [imag] + [pltpu.roll(imag, 32 * k, 1) for k in range(1, 4)]
            seat = 2 * (b % 2)
            zero = jnp.zeros_like(real)
            for p in range(4):
                to_left, to_right = (seat - p) % 4, (seat + 1 - p) % 4
                upper = jnp.where(lane == seat, reals[to_left], jnp.where(lane == seat + 1, imags[to_right], zero))
                lower = jnp.where(lane == seat, imags[to_left], jnp.where(lane == seat + 1, -reals[to_right], zero))
                tile = jnp.concatenate([upper, lower], axis=0).astype(bf16)
                rows = pl.ds(p * 64 + b * 16, 16)
                wide[quad, rows, pl.ds(128 * (b // 2), 128)] = tile
                wide[quad, rows, pl.ds(128 * (1 - b // 2), 128)] = blank

    loop(0, QUADS // 2, widen)

    def near_block(half, step, zz):
        return at(y + step, zz, x) if half == 0 else at(y, zz, x + step)

    def far_block(half, step, yy, zz):
        return at(yy, zz, x + step) if half == 0 else at(y + step, zz, yy)

    for zz in (z, z + 1):
        for half in (0, 1):
            for step in (-1, 1):
                block = near_block(half, step, zz)
                arrived(block, half)
                which = lax.rem(zz, NZ)
                moves = which == (0 if step == -1 else 1)

                @pl.when(moves)
                def _():
                    hop(block, half, 1 if step == -1 else 2, first[half][0 if step == -1 else 1]).start()

                spread_last(block, half)

    loop(QUADS // 2, QUADS, widen)

    for zz in (0, 1):
        for half in (0, 1):
            block = near_block(half, 2, zz)
            arrived(block, half)
            spread_last(block, half)

    def far_pass(i):
        yy, xx, zz = walk(i)
        for half in (0, 1):
            for step in (-1, 1):
                block = far_block(half, step, yy if half == 0 else xx, zz)
                arrived(block, half)

                @pl.when(zz == (0 if step == -1 else 1))
                def _():
                    hop(block, half, 3 if step == -1 else 4, last[half][0 if step == -1 else 1]).start()

                cross(block, half)

    loop(0, NY * NZ, far_pass)

    for a in range(LAGS // 128):
        inverse[:, a * 128 : (a + 1) * 128] = (
            far_cos[:, a : a + 1] * near_cos[...] - far_sin[:, a : a + 1] * near_sin[...]
        ).astype(bf16)

    def cross_near(i):
        yy, xx, zz = walk(i)
        cross(at(yy, zz, x), 0)
        cross(at(y, zz, xx), 1)

    loop(0, NY * NZ, cross_near)

    def far_last(i):
        yy, xx, zz = walk(i)
        for half in (0, 1):
            block = far_block(half, 2, yy if half == 0 else xx, zz)
            arrived(block, half)
            cross(block, half)

    loop(0, NY * NZ, far_last)

    def turn_source(s):
        rows = pl.ds(pl.multiple_of(s * C, C), C)
        for h in range(2):
            flipped = crossed[h, pl.ds(s, QUADS, stride=S), :].T.astype(bf16)
            for k in range(4):
                stacked[rows, (h * 4 + k) * 128 : (h * 4 + k + 1) * 128] = flipped[k * 32 : (k + 1) * 32]

    loop(0, S, turn_source)

    def sent(block, half, slot):
        hop(block, half, slot, z_over).wait_send()

    for half in (0, 1):
        sent(me, half, 0)
        for zz in (0, 1):
            for slot in (1, 2):
                sent(at(y, zz, x), half, slot)
        sent(near_block(half, -1, 0), half, 1)
        sent(near_block(half, 1, 1), half, 2)

    def sent_far(i):
        yy, xx, zz = walk(i)
        for half in (0, 1):
            block = at(yy, zz, x) if half == 0 else at(y, zz, xx)
            sent(block, half, 3)
            sent(block, half, 4)
            along = yy if half == 0 else xx

            @pl.when(zz == 0)
            def _():
                sent(far_block(half, -1, along, 0), half, 3)

            @pl.when(zz == 1)
            def _():
                sent(far_block(half, 1, along, 1), half, 4)


    loop(0, NY * NZ, sent_far)


def turn(bins, steps):
    phase = jnp.mod(bins * steps, L).astype(f32) * (2.0 * math.pi / L)
    return jnp.cos(phase), jnp.sin(phase)


def forward_table():
    bins = K0 + jnp.arange(F, dtype=i32)
    step = 64
    ca, sa = turn(bins[None, :], step * jnp.arange(L // step, dtype=i32)[:, None])
    cb, sb = turn(bins[None, :], jnp.arange(step, dtype=i32)[:, None])
    ca, sa = jnp.concatenate([ca, ca], 1), jnp.concatenate([sa, sa], 1)
    near_cos, near_sin = jnp.concatenate([cb, -sb], 1), jnp.concatenate([sb, cb], 1)
    ca, sa, near_cos, near_sin = lax.optimization_barrier((ca, sa, near_cos, near_sin))
    table = ca[:, None] * near_cos[None] - sa[:, None] * near_sin[None]
    return table.reshape(L, 2 * F).astype(bf16)


def inverse_parts():
    bins = K0 + PACK * jnp.arange(QUADS, dtype=i32)[None, :] + jnp.arange(PACK, dtype=i32)[:, None]
    bins = bins[:, :, None]
    ca, sa = turn(bins, 128 * jnp.arange(LAGS // 128, dtype=i32) - LAGS // 2)
    cb, sb = turn(bins, jnp.arange(128, dtype=i32))
    both = lambda a, b: jnp.stack([a, b], axis=1).reshape(2 * F, a.shape[-1])
    return both(ca, ca), both(sa, sa), both(cb, -sb), both(sb, cb)


def make_band(filter_taps):
    kernel = jnp.concatenate([-filter_taps[:HALO], jnp.ones((1,), bf16), -filter_taps[HALO:]]).astype(f32)
    offset = iota((C, C + 2 * HALO), 1) - iota((C, C + 2 * HALO), 0)
    choose = offset[:, :, None] == jnp.arange(2 * HALO + 1, dtype=i32)
    return jnp.sum(jnp.where(choose, kernel, 0.0), axis=2).astype(bf16)


def lane_order():
    source = jnp.arange(WIN * 2 * W * BINS, dtype=i32)
    group, rest = source // (2 * W * BINS), source % (2 * W * BINS)
    part, rest = rest // (W * BINS), rest % (W * BINS)
    window, one = rest // BINS, rest % BINS
    target = (one // PACK) * 256 + (window % 4) * 64 + (one % PACK) * 16 + part * 8 + group * 2 + window // 4
    lanes = jnp.arange(WIN * 2 * W * BINS, dtype=i32)
    return (target[:, None] == lanes[None, :]).astype(bf16).reshape(WIN, 2 * W * BINS, WIN * 2 * W * BINS)


def per_device(traces, filter_taps, good_channels, source_index):
    keep = good_channels.astype(f32)
    spectrum = mxu(traces.reshape(W * C, L), forward_table())
    spectrum = spectrum.reshape(W, C, 2 * F) * keep[None, :, None]

    bins = jnp.arange(F, dtype=i32)
    near = (jnp.abs(bins[:, None] - bins[None, :]) <= SMOOTH).astype(f32)
    share = 1.0 / jnp.sum(near, axis=0, keepdims=True)
    vmem = pl.BlockSpec(memory_space=pltpu.VMEM)
    dma = pltpu.SemaphoreType.DMA
    quads, own = pl.pallas_call(
        middle,
        out_shape=(
            jax.ShapeDtypeStruct((BINS // PACK, S, 256), bf16),
            jax.ShapeDtypeStruct((WIN, W * C, 2 * F), bf16),
        ),
        in_specs=[vmem] * 7,
        out_specs=(vmem, vmem),
        scratch_shapes=[
            pltpu.VMEM((W, HALO, 2 * F), f32),
            pltpu.VMEM((W, HALO, 2 * F), f32),
            pltpu.VMEM((W, C, 2 * F), f32),
            pltpu.VMEM((BLK, C, 2 * W * BINS), bf16),
            pltpu.VMEM((BLK, C, 2 * W * BINS), bf16),
            pltpu.VMEM((WIN, S, 2 * W * BINS), bf16),
            pltpu.VMEM((WIN, S, 2 * W * BINS), bf16),
            dma((2, W)), dma((2, W)), dma((BLK,)), dma((BLK,)),
            dma((WIN,)), dma((WIN,)), dma((WIN,)), dma((WIN,)),
        ],
        compiler_params=pltpu.CompilerParams(
            collective_id=0, has_side_effects=True, vmem_limit_bytes=24 << 20
        ),
        name="middle",
    )(
        spectrum, keep[:, None], make_band(filter_taps), near.astype(bf16), share,
        source_index.astype(i32)[:, None], lane_order(),
    )

    halves = 2
    stacked, inverse = pl.pallas_call(
        gather_cross,
        out_shape=(
            jax.ShapeDtypeStruct((S * C, 2 * F), bf16),
            jax.ShapeDtypeStruct((2 * F, LAGS), bf16),
        ),
        in_specs=[vmem] * 6,
        out_specs=(vmem, vmem),
        scratch_shapes=[
            pltpu.VMEM((BLK, BINS // PACK, S, 256), bf16),
            pltpu.VMEM((F * 16, 128), f32),
            pltpu.VMEM((QUADS, 256, 256), bf16),
            pltpu.VMEM((2, QUADS * S, 128), f32),
            dma((BLK, halves, 5)), dma((BLK, halves)),
        ],
        compiler_params=pltpu.CompilerParams(
            collective_id=1, has_side_effects=True, vmem_limit_bytes=56 << 20
        ),
        name="gather_cross",
    )(quads, own.reshape(WIN * W * C, 2 * F), *inverse_parts())

    scaling = 1.0 / math.sqrt(F * W * WIN)
    lagged = mxu(stacked, inverse) * scaling
    return lagged.reshape(S, C, LAGS)


def solution(mesh):
    placed = (P("win", "chan", None), P(), P("chan"), P())
    return jax.shard_map(
        per_device, mesh=mesh, in_specs=placed, out_specs=P("win", "chan", None), check_vma=False
    )
```

```python
import functools
import math

import jax
import jax.numpy as jnp
from jax import lax
from jax.experimental import pallas as pl
from jax.experimental.pallas import tpu as pltpu
from jax.sharding import PartitionSpec as P

L = 7680
F = 512
LAGS = 2048
HALO = 16
SMOOTH = 64
K0 = 31

WIN = 4
BLK = 32
NX = 4
NZ = 2
NY = 4
W = 8
C = 32
S = 64
BINS = F // BLK
QUADS = F // 4
PACK = 4
PAIR = 2
DEEP = 2 * W * WIN
MESH = pl.DeviceIdType.MESH
f32, bf16, i32 = jnp.float32, jnp.bfloat16, jnp.int32


def iota(shape, dim):
    return lax.broadcasted_iota(i32, shape, dim)


def mxu(a, b):
    return jnp.dot(a, b, preferred_element_type=f32)


def loop(start, stop, body):
    def step(i, carry):
        body(i)
        return carry

    lax.fori_loop(start, stop, step, 0)


def thirds(x):
    high = x.astype(bf16)
    rest = x - high.astype(f32)
    middle = rest.astype(bf16)
    low = (rest - middle.astype(f32)).astype(bf16)
    return high, middle, low


def chan_copy(src, dst, send, recv, peer):
    return pltpu.make_async_remote_copy(
        src_ref=src, dst_ref=dst, send_sem=send, recv_sem=recv,
        device_id=(lax.axis_index("win"), peer), device_id_type=MESH,
    )


def win_copy(src, dst, send, recv, peer):
    return pltpu.make_async_remote_copy(
        src_ref=src, dst_ref=dst, send_sem=send, recv_sem=recv,
        device_id=(peer, lax.axis_index("chan")), device_id_type=MESH,
    )


def diagonal(row, count):
    return jnp.sum(jnp.where(iota((count, count), 0) == iota((count, count), 1), row, 0.0), axis=1, keepdims=True)


def whole(
    spec, good, taps, near, share, sources, order, far_cos, far_sin, near_cos, near_sin, crossed_hbm, inverse_hbm,
    low, high, white, outgoing, mixed, chosen, regroup, own, quads, held, turned, wide, crossed, inverse,
    halo_send, halo_recv, all_send, all_recv, own_send, own_recv, win_send, win_recv, send, recv, out_sem,
):
    me = lax.axis_index("chan")
    group = lax.axis_index("win")
    y, z, x = me // (NZ * NX), lax.rem(me // NX, NZ), lax.rem(me, NX)
    layer, core = group // 2, lax.rem(group, 2)
    sibling, across, diagonal_group = layer * 2 + 1 - core, (1 - layer) * 2 + core, (1 - layer) * 2 + 1 - core

    barrier = pltpu.get_barrier_semaphore()

    def greet_chan(k):
        pl.semaphore_signal(barrier, inc=1, device_id=(group, lax.rem(me + k, BLK)), device_id_type=MESH)

    def greet_win(k):
        pl.semaphore_signal(barrier, inc=1, device_id=(lax.rem(group + k, WIN), me), device_id_type=MESH)

    loop(1, BLK, greet_chan)
    loop(1, WIN, greet_win)
    pl.semaphore_wait(barrier, BLK + WIN - 2)

    right, left = lax.rem(me + 1, BLK), lax.rem(me + BLK - 1, BLK)

    def to_right(w):
        return chan_copy(spec.at[w, pl.ds(C - HALO, HALO)], low.at[w], halo_send.at[0, w], halo_recv.at[0, w], right)

    def to_left(w):
        return chan_copy(spec.at[w, pl.ds(0, HALO)], high.at[w], halo_send.at[1, w], halo_recv.at[1, w], left)

    def send_halo(w):
        @pl.when(me < BLK - 1)
        def _():
            to_right(w).start()

        @pl.when(me > 0)
        def _():
            to_left(w).start()

    loop(0, W, send_halo)

    @pl.when(me == 0)
    def _():
        low[...] = jnp.zeros_like(low)

    @pl.when(me == BLK - 1)
    def _():
        high[...] = jnp.zeros_like(high)

    for b in range(PACK):
        bins = slice(b * QUADS, (b + 1) * QUADS)
        fc, fs = far_cos[:, bins].T, far_sin[:, bins].T
        nc, ns = near_cos[bins, :], near_sin[bins, :]
        for a in range(LAGS // 128):
            columns = slice(a * 128, (a + 1) * 128)
            ca, sa = fc[:, a : a + 1], fs[:, a : a + 1]
            inverse[2 * b * QUADS : (2 * b + 1) * QUADS, columns] = (ca * nc - sa * ns).astype(bf16)
            inverse[(2 * b + 1) * QUADS : (2 * b + 2) * QUADS, columns] = -(sa * nc + ca * ns).astype(bf16)
    inverse_out = pltpu.make_async_copy(inverse, inverse_hbm, out_sem.at[0])
    inverse_out.start()

    offset = iota((C, C + 2 * HALO), 1) - iota((C, C + 2 * HALO), 0)
    band = jnp.where(offset == HALO, 1.0, 0.0)
    for o in range(HALO):
        band = jnp.where(offset == o, -taps[o], band)
        band = jnp.where(offset == HALO + 1 + o, -taps[HALO + o], band)
    band = band.astype(bf16)
    keep = diagonal(good[...].astype(f32), C)

    def to_group(hop, w, whose, peer):
        rows = pl.ds(pl.multiple_of(w * C, C), C)
        return win_copy(own.at[whose, rows], own.at[whose, rows], own_send.at[hop, w], own_recv.at[hop, w], peer)

    def window(w):
        @pl.when(me > 0)
        def _():
            to_right(w).wait_recv()

        @pl.when(me < BLK - 1)
        def _():
            to_left(w).wait_recv()

        padded = jnp.concatenate([low[w], spec[w], high[w]], axis=0)
        parts = thirds(padded)
        filtered = (mxu(band, parts[0]) + mxu(band, parts[1]) + mxu(band, parts[2])) * keep
        real, imag = filtered[:, :F], filtered[:, F:]
        magnitude = jnp.sqrt(real * real + imag * imag)
        sums = mxu(jnp.concatenate(thirds(magnitude), axis=0), near[...])
        amplitude = (sums[:C] + sums[C : 2 * C] + sums[2 * C :]) * share[...]
        divisor = amplitude + 1e-06
        out = jnp.concatenate([real / divisor, imag / divisor], axis=1)
        white[w] = out
        own[group, pl.ds(pl.multiple_of(w * C, C), C), :] = out.astype(bf16)
        to_group(0, w, group, across).start()
        to_group(1, w, group, sibling).start()

    loop(0, W, window)

    tiles = F // 128
    per_tile = 128 // BINS
    lane = iota((C, 128), 1) // BINS

    def regroup_tile(t):
        part, tile = t // tiles, lax.rem(t, tiles)
        columns = pl.ds(pl.multiple_of(t * 128, 128), 128)
        values = [white[w, :, columns] for w in range(W)]
        for m in range(per_tile):
            total = jnp.zeros((C, 128), f32)
            for w in range(W):
                shift = (w - m) * BINS % 128
                moved = pltpu.roll(values[w], shift, 1) if shift else values[w]
                total = jnp.where(lane == w, moved, total)
            outgoing[tile * per_tile + m, :, pl.ds(pl.multiple_of(part * 128, 128), 128)] = total.astype(bf16)

    loop(0, 2 * tiles, regroup_tile)

    def exchange(k):
        peer = lax.rem(me + k, BLK)
        return chan_copy(outgoing.at[peer], mixed.at[me], all_send.at[k], all_recv.at[k], peer)

    loop(1, BLK, lambda k: exchange(k).start())
    mixed[me] = outgoing[me]

    def turn_group(whose):
        def turn_tile(part_tile):
            part, tile = part_tile // tiles, lax.rem(part_tile, tiles)
            columns = pl.ds(pl.multiple_of(part_tile * 128, 128), 128)
            for half in range(2):
                block = own[whose, half * 128 : (half + 1) * 128, columns]
                start = tile * 128 * 16 + part * 8 + whose * 2 + half
                turned[pl.ds(start, 128, stride=16), :] = block.astype(f32).T

        loop(0, 2 * tiles, turn_tile)

    turn_group(group)
    wanted = jnp.where(iota((WIN * S, BLK * C), 1) == diagonal(sources[...].astype(f32), WIN * S).astype(i32), 1.0, 0.0).astype(bf16)
    loop(0, W, lambda w: to_group(1, w, sibling, sibling).wait_recv())
    turn_group(sibling)

    loop(1, BLK, lambda k: exchange(k).wait_recv())
    picked = mxu(wanted, mixed[...].reshape(BLK * C, 2 * W * BINS)).astype(bf16)
    chosen[...] = picked.reshape(WIN, S, 2 * W * BINS)

    def trade(k):
        peer = lax.rem(group + k, WIN)
        return win_copy(chosen.at[peer], regroup.at[group], win_send.at[k], win_recv.at[k], peer)

    loop(1, WIN, lambda k: trade(k).start())
    regroup[group] = chosen[group]

    def relay(w):
        to_group(0, w, across, across).wait_recv()
        to_group(2, w, across, sibling).start()

    loop(0, W, relay)
    turn_group(across)
    loop(1, WIN, lambda k: trade(k).wait_recv())
    arranged = mxu(regroup[0], order[0])
    for g in range(1, WIN):
        arranged += mxu(regroup[g], order[g])
    for q in range(BINS // PACK):
        quads[q] = arranged[:, q * 256 : (q + 1) * 256].astype(bf16)

    def at(yy, zz, xx):
        return (lax.rem(yy + NY, NY) * NZ + lax.rem(zz, NZ)) * NX + lax.rem(xx + NX, NX)

    y_up, y_down, x_up, x_down, z_over = at(y + 1, z, x), at(y - 1, z, x), at(y, z, x + 1), at(y, z, x - 1), at(y, z + 1, x)

    first = ((y_up, y_down), (x_up, x_down))
    last = ((x_up, x_down), (y_up, y_down))
    per_half = BINS // PACK // 2

    def piece(block, half):
        return held.at[block, pl.ds(half * per_half, per_half)]

    def hop(block, half, slot, peer, src=None):
        src = piece(block, half) if src is None else src
        return chan_copy(src, piece(block, half), send.at[block, half, slot], recv.at[block, half], peer)

    def own_piece(half):
        return quads.at[pl.ds(half * per_half, per_half)]

    def arrived(block, half):
        hop(block, half, 0, z_over).wait_recv()

    def spread_last(block, half, src=None):
        hop(block, half, 3, last[half][0], src).start()
        hop(block, half, 4, last[half][1], src).start()

    def spread(block, half, src=None):
        hop(block, half, 1, first[half][0], src).start()
        hop(block, half, 2, first[half][1], src).start()
        spread_last(block, half, src)

    def walk(i):
        k = i // NZ
        k = jnp.where(k > 1, 5 - k, k)
        return lax.rem(y + k, NY), lax.rem(x + k, NX), lax.rem(i, NZ)

    for half in (0, 1):
        hop(me, half, 0, z_over, own_piece(half)).start()
    for half in (0, 1):
        spread(me, half, own_piece(half))
    for q in range(2 * per_half):
        held[me, q] = quads[q]

    loop(0, W, lambda w: to_group(2, w, diagonal_group, sibling).wait_recv())
    turn_group(diagonal_group)

    for half in (0, 1):
        arrived(z_over, half)
        spread(z_over, half)

    lane32 = iota((16, 128), 1) // 32
    seats = [jnp.where(lane32 == k, 1.0, 0.0).astype(bf16) for k in range(4)]

    def widen(quad):
        for b in range(PACK):
            base = pl.multiple_of((quad * PACK + b) * 16, 16)
            real, imag = turned[pl.ds(base, 8), :], turned[pl.ds(base + 8, 8), :]
            straight, crosswise = [], []
            for k in range(4):
                r = pltpu.roll(real, 32 * k, 1) if k else real
                i = pltpu.roll(imag, 32 * k, 1) if k else imag
                straight.append(jnp.concatenate([r, i], axis=0).astype(bf16))
                crosswise.append(jnp.concatenate([i, -r], axis=0).astype(bf16))
            seat = 2 * (b % PAIR)
            for p in range(4):
                tile = straight[(seat - p) % 4] * seats[seat] + crosswise[(seat + 1 - p) % 4] * seats[seat + 1]
                wide[quad * 2 + b // PAIR, pl.ds(p * 32 + (b % PAIR) * 16, 16), :] = tile

    loop(0, QUADS, widen)

    def result_out(first_row, count):
        rows = pl.ds(pl.multiple_of(first_row, S), count)
        return pltpu.make_async_copy(crossed.at[:, rows], crossed_hbm.at[:, rows], out_sem.at[1])

    def cross(block, half):
        for j in range(per_half):
            quad = block * (2 * per_half) + half * per_half + j
            rows = pl.ds(pl.multiple_of(quad * S, S), S)
            for h in range(2):
                crossed[h, rows, :] = mxu(held[block, half * per_half + j, :, h * 128 : (h + 1) * 128], wide[quad * 2 + h])
        result_out((block * 2 + half) * per_half * S, per_half * S).start()

    def near_block(half, step, zz):
        return at(y + step, zz, x) if half == 0 else at(y, zz, x + step)

    def far_block(half, step, along, zz):
        return at(along, zz, x + step) if half == 0 else at(y + step, zz, along)

    for zz in (z, z + 1):
        for half in (0, 1):
            for step in (-1, 1):
                block = near_block(half, step, zz)
                arrived(block, half)

                @pl.when(lax.rem(zz, NZ) == (0 if step == -1 else 1))
                def _():
                    hop(block, half, 1 if step == -1 else 2, first[half][0 if step == -1 else 1]).start()

                spread_last(block, half)

    for zz in (0, 1):
        for half in (0, 1):
            block = near_block(half, 2, zz)
            arrived(block, half)
            spread_last(block, half)

    def far_pass(i):
        yy, xx, zz = walk(i)
        for half in (0, 1):
            for step in (-1, 1):
                block = far_block(half, step, yy if half == 0 else xx, zz)
                arrived(block, half)

                @pl.when(zz == (0 if step == -1 else 1))
                def _():
                    hop(block, half, 3 if step == -1 else 4, last[half][0 if step == -1 else 1]).start()

                cross(block, half)

    loop(0, NY * NZ, far_pass)

    def cross_near(i):
        yy, xx, zz = walk(i)
        cross(at(yy, zz, x), 0)
        cross(at(y, zz, xx), 1)

    loop(0, NY * NZ, cross_near)

    def far_last(i):
        yy, xx, zz = walk(i)
        for half in (0, 1):
            block = far_block(half, 2, yy if half == 0 else xx, zz)
            arrived(block, half)
            cross(block, half)

    loop(0, NY * NZ, far_last)

    def finish_win(k):
        trade(k).wait_send()

    def finish_own(w):
        to_group(0, w, group, across).wait_send()
        to_group(1, w, group, sibling).wait_send()
        to_group(2, w, across, sibling).wait_send()

    def finish_halo(w):
        @pl.when(me < BLK - 1)
        def _():
            to_right(w).wait_send()

        @pl.when(me > 0)
        def _():
            to_left(w).wait_send()

    loop(1, WIN, finish_win)
    loop(0, W, finish_own)
    loop(1, BLK, lambda k: exchange(k).wait_send())
    loop(0, W, finish_halo)

    def sent(block, half, slot):
        hop(block, half, slot, z_over).wait_send()

    for half in (0, 1):
        sent(me, half, 0)
        for zz in (0, 1):
            for slot in (1, 2):
                sent(at(y, zz, x), half, slot)
        sent(near_block(half, -1, 0), half, 1)
        sent(near_block(half, 1, 1), half, 2)

    def sent_far(i):
        yy, xx, zz = walk(i)
        for half in (0, 1):
            block = at(yy, zz, x) if half == 0 else at(y, zz, xx)
            sent(block, half, 3)
            sent(block, half, 4)
            along = yy if half == 0 else xx

            @pl.when(zz == 0)
            def _():
                sent(far_block(half, -1, along, 0), half, 3)

            @pl.when(zz == 1)
            def _():
                sent(far_block(half, 1, along, 1), half, 4)

    loop(0, NY * NZ, sent_far)
    inverse_out.wait()
    result_out(0, QUADS * S).wait()


def to_lags(scaling, crossed, inverse, out, stacked):
    for s in range(8):
        for h in range(2):
            flipped = crossed[h, :, s, :].T.astype(bf16)
            for k in range(4):
                stacked[s * C : (s + 1) * C, (h * 4 + k) * 128 : (h * 4 + k + 1) * 128] = flipped[k * 32 : (k + 1) * 32]
    out[...] = (mxu(stacked[...], inverse[...]) * scaling).reshape(8, C, LAGS)


def turn(bins, steps):
    phase = jnp.mod(bins * steps, L).astype(f32) * (2.0 * math.pi / L)
    return jnp.cos(phase), jnp.sin(phase)


def forward_table():
    bins = K0 + jnp.arange(F, dtype=i32)
    step = 64
    ca, sa = turn(bins[None, :], step * jnp.arange(L // step, dtype=i32)[:, None])
    cb, sb = turn(bins[None, :], jnp.arange(step, dtype=i32)[:, None])
    ca, sa = jnp.concatenate([ca, ca], 1), jnp.concatenate([sa, sa], 1)
    near_cos, near_sin = jnp.concatenate([cb, -sb], 1), jnp.concatenate([sb, cb], 1)
    ca, sa, near_cos, near_sin = lax.optimization_barrier((ca, sa, near_cos, near_sin))
    table = ca[:, None] * near_cos[None] - sa[:, None] * near_sin[None]
    return table.reshape(L, 2 * F).astype(bf16)


def inverse_parts():
    bins = (K0 + PACK * jnp.arange(QUADS, dtype=i32)[None, :] + jnp.arange(PACK, dtype=i32)[:, None]).reshape(F)
    far = turn(bins[None, :], 128 * jnp.arange(LAGS // 128, dtype=i32)[:, None] - LAGS // 2)
    return far + turn(bins[:, None], jnp.arange(128, dtype=i32)[None, :])


def lane_order():
    source = jnp.arange(WIN * 2 * W * BINS, dtype=i32)
    group, rest = source // (2 * W * BINS), source % (2 * W * BINS)
    part, rest = rest // (W * BINS), rest % (W * BINS)
    window, one = rest // BINS, rest % BINS
    target = (one // PAIR) * 128 + (window % 4) * 32 + (one % PAIR) * 16 + part * 8 + group * 2 + window // 4
    lanes = jnp.arange(WIN * 2 * W * BINS, dtype=i32)
    return (target[:, None] == lanes[None, :]).astype(bf16).reshape(WIN, 2 * W * BINS, WIN * 2 * W * BINS)


def per_device(traces, filter_taps, good_channels, source_index):
    keep = good_channels.astype(f32)
    spectrum = mxu(traces.reshape(W * C, L), forward_table())
    spectrum = spectrum.reshape(W, C, 2 * F) * keep[None, :, None]

    bins = jnp.arange(F, dtype=i32)
    near = (jnp.abs(bins[:, None] - bins[None, :]) <= SMOOTH).astype(f32)
    share = 1.0 / jnp.sum(near, axis=0, keepdims=True)
    vmem = pl.BlockSpec(memory_space=pltpu.VMEM)
    smem = pl.BlockSpec(memory_space=pltpu.SMEM)
    anywhere = pl.BlockSpec(memory_space=pl.ANY)
    dma = pltpu.SemaphoreType.DMA
    crossed, inverse = pl.pallas_call(
        whole,
        out_shape=(
            jax.ShapeDtypeStruct((2, QUADS * S, 128), f32),
            jax.ShapeDtypeStruct((2 * F, LAGS), bf16),
        ),
        in_specs=[vmem, vmem, smem] + [vmem] * 8,
        out_specs=(anywhere, anywhere),
        scratch_shapes=[
            pltpu.VMEM((W, HALO, 2 * F), f32),
            pltpu.VMEM((W, HALO, 2 * F), f32),
            pltpu.VMEM((W, C, 2 * F), f32),
            pltpu.VMEM((BLK, C, 2 * W * BINS), bf16),
            pltpu.VMEM((BLK, C, 2 * W * BINS), bf16),
            pltpu.VMEM((WIN, S, 2 * W * BINS), bf16),
            pltpu.VMEM((WIN, S, 2 * W * BINS), bf16),
            pltpu.VMEM((WIN, W * C, 2 * F), bf16),
            pltpu.VMEM((BINS // PACK, S, 256), bf16),
            pltpu.VMEM((BLK, BINS // PACK, S, 256), bf16),
            pltpu.VMEM((F * 16, 128), f32),
            pltpu.VMEM((QUADS * 2, 128, 128), bf16),
            pltpu.VMEM((2, QUADS * S, 128), f32),
            pltpu.VMEM((2 * F, LAGS), bf16),
            dma((2, W)), dma((2, W)), dma((BLK,)), dma((BLK,)),
            dma((3, W)), dma((3, W)), dma((WIN,)), dma((WIN,)),
            dma((BLK, 2, 5)), dma((BLK, 2)), dma((2,)),
        ],
        compiler_params=pltpu.CompilerParams(
            collective_id=0, has_side_effects=True, vmem_limit_bytes=52 << 20
        ),
        name="whole",
    )(
        spectrum, good_channels.astype(i32)[None, :], filter_taps.astype(f32), near.astype(bf16), share,
        source_index.astype(i32)[None, :], lane_order(), *inverse_parts(),
    )

    return pl.pallas_call(
        functools.partial(to_lags, 1.0 / math.sqrt(F * W * WIN)),
        grid=(S // 8,),
        out_shape=jax.ShapeDtypeStruct((S, C, LAGS), f32),
        in_specs=[
            pl.BlockSpec((2, QUADS, 8, 128), lambda i: (0, 0, i, 0)),
            pl.BlockSpec((2 * F, LAGS), lambda i: (0, 0), pipeline_mode=pl.Buffered(1)),
        ],
        out_specs=pl.BlockSpec((8, C, LAGS), lambda i: (i, 0, 0)),
        scratch_shapes=[pltpu.VMEM((8 * C, 2 * F), bf16)],
        compiler_params=pltpu.CompilerParams(vmem_limit_bytes=32 << 20),
        name="to_lags",
    )(crossed.reshape(2, QUADS, S, 128), inverse)


def solution(mesh):
    placed = (P("win", "chan", None), P(), P("chan"), P())
    return jax.shard_map(
        per_device, mesh=mesh, in_specs=placed, out_specs=P("win", "chan", None), check_vma=False
    )
```

```python
import functools
import math

import jax
import jax.numpy as jnp
from jax import lax
from jax.experimental import pallas as pl
from jax.experimental.pallas import tpu as pltpu
from jax.sharding import PartitionSpec as P

L = 7680
F = 512
LAGS = 2048
HALO = 16
SMOOTH = 64
K0 = 31

WIN = 4
BLK = 32
NX = 4
NZ = 2
NY = 4
W = 8
C = 32
S = 64
BINS = F // BLK
QUADS = F // 4
PACK = 4
PAIR = 2
STEP = 64
DEEP = 2 * W * WIN
MESH = pl.DeviceIdType.MESH
f32, bf16, i32 = jnp.float32, jnp.bfloat16, jnp.int32


def iota(shape, dim):
    return lax.broadcasted_iota(i32, shape, dim)


def mxu(a, b):
    return jnp.dot(a, b, preferred_element_type=f32)


def loop(start, stop, body):
    def step(i, carry):
        body(i)
        return carry

    lax.fori_loop(start, stop, step, 0)


def thirds(x):
    high = x.astype(bf16)
    rest = x - high.astype(f32)
    middle = rest.astype(bf16)
    low = (rest - middle.astype(f32)).astype(bf16)
    return high, middle, low


def chan_copy(src, dst, send, recv, peer):
    return pltpu.make_async_remote_copy(
        src_ref=src, dst_ref=dst, send_sem=send, recv_sem=recv,
        device_id=(lax.axis_index("win"), peer), device_id_type=MESH,
    )


def win_copy(src, dst, send, recv, peer):
    return pltpu.make_async_remote_copy(
        src_ref=src, dst_ref=dst, send_sem=send, recv_sem=recv,
        device_id=(peer, lax.axis_index("chan")), device_id_type=MESH,
    )


def diagonal(row, count):
    return jnp.sum(jnp.where(iota((count, count), 0) == iota((count, count), 1), row, 0.0), axis=1, keepdims=True)


def whole(
    traces, good, taps, sources, row_cos, row_sin, step_cos, step_sin, far_cos, far_sin, near_cos, near_sin,
    crossed_hbm, inverse_hbm,
    rows, table, spec, low, high, filtered, magnitudes, outgoing, mixed, chosen, regroup, own, quads, held, turned, wide,
    crossed, inverse,
    halo_send, halo_recv, all_send, all_recv, own_send, own_recv, win_send, win_recv, send, recv, out_sem,
):
    me = lax.axis_index("chan")
    group = lax.axis_index("win")
    y, z, x = me // (NZ * NX), lax.rem(me // NX, NZ), lax.rem(me, NX)
    layer, core = group // 2, lax.rem(group, 2)
    sibling, across, diagonal_group = layer * 2 + 1 - core, (1 - layer) * 2 + core, (1 - layer) * 2 + 1 - core

    rows_in = pltpu.make_async_copy(traces, rows, out_sem.at[2])
    rows_in.start()
    barrier = pltpu.get_barrier_semaphore()

    def greet_chan(k):
        pl.semaphore_signal(barrier, inc=1, device_id=(group, lax.rem(me + k, BLK)), device_id_type=MESH)

    def greet_win(k):
        pl.semaphore_signal(barrier, inc=1, device_id=(lax.rem(group + k, WIN), me), device_id_type=MESH)

    loop(1, BLK, greet_chan)
    loop(1, WIN, greet_win)

    offset = iota((C, C + 2 * HALO), 1) - iota((C, C + 2 * HALO), 0)
    weights = taps[...].astype(f32)
    band = jnp.where(offset == HALO, 1.0, 0.0)
    for o in range(HALO):
        band = jnp.where(offset == o, -weights[:, o : o + 1], band)
        band = jnp.where(offset == HALO + 1 + o, -weights[:, HALO + o : HALO + o + 1], band)
    band = jnp.concatenate([band, band, band], axis=1).astype(bf16)
    keep = diagonal(good[...].astype(f32), C)
    beside = jnp.where(jnp.abs(iota((384, 128), 0) - 128 - iota((384, 128), 1)) <= SMOOTH, 1.0, 0.0).astype(bf16)
    magnitudes[:, 0:128] = jnp.zeros((3 * W * C, 128), bf16)
    magnitudes[:, 640:768] = jnp.zeros((3 * W * C, 128), bf16)

    @pl.when(me == 0)
    def _():
        low[...] = jnp.zeros_like(low)

    @pl.when(me == BLK - 1)
    def _():
        high[...] = jnp.zeros_like(high)

    tiles = F // 128
    per_tile = 128 // BINS
    right, left = lax.rem(me + 1, BLK), lax.rem(me + BLK - 1, BLK)

    def to_right(n):
        return chan_copy(spec.at[n, :, pl.ds(C - HALO, HALO)], low.at[n], halo_send.at[0, n], halo_recv.at[0, n], right)

    def to_left(n):
        return chan_copy(spec.at[n, :, pl.ds(0, HALO)], high.at[n], halo_send.at[1, n], halo_recv.at[1, n], left)

    def tile_of(n):
        return pl.ds(pl.multiple_of(n * 128, 128), 128)

    def transform(n):
        columns = tile_of(n)
        cb, sb = step_cos[:, columns], step_sin[:, columns]

        def table_rows(i):
            eight = pl.ds(pl.multiple_of(i * 8, 8), 8)
            cas, sas = row_cos[eight, columns], row_sin[eight, columns]
            for u in range(8):
                ca, sa = cas[u : u + 1], sas[u : u + 1]
                at_rows = pl.ds(pl.multiple_of((i * 8 + u) * STEP, STEP), STEP)
                table[at_rows, 0:128] = (ca * cb - sa * sb).astype(bf16)
                table[at_rows, 128:256] = (-sa * cb - ca * sb).astype(bf16)

        loop(0, L // STEP // 8, table_rows)

        @pl.when(n == 0)
        def _():
            rows_in.wait()

        spec[n] = mxu(rows[...], table[...]).reshape(W, C, 256) * keep

        @pl.when(n == 0)
        def _():
            pl.semaphore_wait(barrier, BLK + WIN - 2)

        @pl.when(me < BLK - 1)
        def _():
            to_right(n).start()

        @pl.when(me > 0)
        def _():
            to_left(n).start()

    def filter_tile(n):
        @pl.when(me > 0)
        def _():
            to_right(n).wait_recv()

        @pl.when(me < BLK - 1)
        def _():
            to_left(n).wait_recv()

        for w in range(W):
            padded = jnp.concatenate([low[n, w], spec[n, w], high[n, w]], axis=0)
            out = mxu(band, jnp.concatenate(thirds(padded), axis=0)) * keep
            filtered[n, w * C : (w + 1) * C, :] = out
            real, imag = out[:, :128], out[:, 128:]
            for k, part in enumerate(thirds(jnp.sqrt(real * real + imag * imag))):
                magnitudes[(k * W + w) * C : (k * W + w + 1) * C, tile_of(n + 1)] = part

    lane = iota((C, 128), 1) // BINS

    def exchange(k):
        peer = lax.rem(me + k, BLK)
        return chan_copy(outgoing.at[peer], mixed.at[me], all_send.at[k], all_recv.at[k], peer)

    def to_group(hop, tile, whose, peer):
        return win_copy(own.at[whose, tile], own.at[whose, tile], own_send.at[hop, tile], own_recv.at[hop, tile], peer)

    def turn_tile(whose, part, tile):
        for half in range(2):
            block = own[whose, part * tiles + tile, half * 128 : (half + 1) * 128, :]
            start = tile * 128 * 16 + part * 8 + whose * 2 + half
            turned[pl.ds(start, 128, stride=16), :] = block.astype(f32).T

    def turn_group(whose):
        def both(tile):
            turn_tile(whose, 0, tile)
            turn_tile(whose, 1, tile)

        loop(0, tiles, both)

    def home(n, m):
        return (m // NZ) * NZ * NX + (m % NZ) * NX + lax.rem(n + m // NZ, NX)

    def place(block):
        yy, zz, xx = block // (NZ * NX), lax.rem(block // NX, NZ), lax.rem(block, NX)
        return lax.rem(xx - yy + NX, NX) * per_tile + yy * NZ + zz

    def whiten_tile(n):
        sums = mxu(magnitudes[:, pl.ds(pl.multiple_of(n * 128, 128), 384)], beside)
        bins = iota((1, 128), 1) + n * 128
        count = 1 + jnp.minimum(bins, SMOOTH) + jnp.minimum(F - 1 - bins, SMOOTH)
        total = sums[: W * C] + sums[W * C : 2 * W * C] + sums[2 * W * C :]
        inverse_amplitude = 1.0 / (total * (1.0 / count.astype(f32)) + 1e-06)
        for part in range(2):
            values = filtered[n, :, part * 128 : (part + 1) * 128] * inverse_amplitude
            own[group, part * tiles + n] = values.astype(bf16)
            windows = [values[w * C : (w + 1) * C] for w in range(W)]
            for m in range(per_tile):
                packed = jnp.zeros((C, 128), f32)
                for w in range(W):
                    shift = (w - m) * BINS % 128
                    moved = pltpu.roll(windows[w], shift, 1) if shift else windows[w]
                    packed = jnp.where(lane == w, moved, packed)
                outgoing[home(n, m), :, part * 128 : (part + 1) * 128] = packed.astype(bf16)
        for m in range(per_tile):
            peer = home(n, m)

            @pl.when(peer != me)
            def _():
                exchange(lax.rem(peer - me + BLK, BLK)).start()

        for part in range(2):
            to_group(0, part * tiles + n, group, across).start()
            to_group(1, part * tiles + n, group, sibling).start()

    def stage(n):
        @pl.when(n < tiles)
        def _():
            transform(n)

        @pl.when((n >= 2) & (n < tiles + 2))
        def _():
            filter_tile(n - 2)

        @pl.when(n >= 3)
        def _():
            whiten_tile(n - 3)

    loop(0, tiles + 3, stage)
    mixed[me] = outgoing[me]

    wanted = jnp.where(iota((WIN * S, BLK * C), 1) == diagonal(sources[...].astype(f32), WIN * S).astype(i32), 1.0, 0.0).astype(bf16)
    span = 2 * W * BINS
    source = iota((span, 1), 0)
    window, one = lax.rem(source // BINS, W), lax.rem(source, BINS)
    target = (one // PAIR) * 128 + lax.rem(window, 4) * 32 + lax.rem(one, PAIR) * 16 + source // (W * BINS) * 8 + window // 4
    order = jnp.where(iota((span, WIN * span), 1) == target, 1.0, 0.0).astype(bf16)
    turn_group(group)
    loop(0, 2 * tiles, lambda t: to_group(1, t, sibling, sibling).wait_recv())
    turn_group(sibling)

    loop(1, BLK, lambda k: exchange(k).wait_recv())
    picked = mxu(wanted, mixed[...].reshape(BLK * C, 2 * W * BINS)).astype(bf16)
    chosen[...] = picked.reshape(WIN, S, 2 * W * BINS)

    def trade(k):
        peer = lax.rem(group + k, WIN)
        return win_copy(chosen.at[peer], regroup.at[group], win_send.at[k], win_recv.at[k], peer)

    loop(1, WIN, lambda k: trade(k).start())
    regroup[group] = chosen[group]

    def relay(t):
        to_group(0, t, across, across).wait_recv()
        to_group(2, t, across, sibling).start()

    loop(0, 2 * tiles, relay)
    turn_group(across)
    loop(1, WIN, lambda k: trade(k).wait_recv())
    arranged = mxu(regroup[0], order)
    for g in range(1, WIN):
        arranged += pltpu.roll(mxu(regroup[g], order), 2 * g, 1)
    for q in range(BINS // PACK):
        quads[q] = arranged[:, q * 256 : (q + 1) * 256].astype(bf16)

    def at(yy, zz, xx):
        return (lax.rem(yy + NY, NY) * NZ + lax.rem(zz, NZ)) * NX + lax.rem(xx + NX, NX)

    y_up, y_down, x_up, x_down, z_over = at(y + 1, z, x), at(y - 1, z, x), at(y, z, x + 1), at(y, z, x - 1), at(y, z + 1, x)

    first = ((y_up, y_down), (x_up, x_down))
    last = ((x_up, x_down), (y_up, y_down))
    per_half = BINS // PACK // 2

    def piece(block, half):
        return held.at[block, pl.ds(half * per_half, per_half)]

    def hop(block, half, slot, peer, src=None):
        src = piece(block, half) if src is None else src
        return chan_copy(src, piece(block, half), send.at[block, half, slot], recv.at[block, half], peer)

    def own_piece(half):
        return quads.at[pl.ds(half * per_half, per_half)]

    def arrived(block, half):
        hop(block, half, 0, z_over).wait_recv()

    def spread_last(block, half, src=None):
        hop(block, half, 3, last[half][0], src).start()
        hop(block, half, 4, last[half][1], src).start()

    def spread(block, half, src=None):
        hop(block, half, 1, first[half][0], src).start()
        hop(block, half, 2, first[half][1], src).start()
        spread_last(block, half, src)

    def walk(i):
        k = i // NZ
        k = jnp.where(k > 1, 5 - k, k)
        return lax.rem(y + k, NY), lax.rem(x + k, NX), lax.rem(i, NZ)

    for half in (0, 1):
        hop(me, half, 0, z_over, own_piece(half)).start()
    for half in (0, 1):
        spread(me, half, own_piece(half))
    for q in range(2 * per_half):
        held[me, q] = quads[q]

    loop(0, 2 * tiles, lambda t: to_group(2, t, diagonal_group, sibling).wait_recv())
    turn_group(diagonal_group)

    for half in (0, 1):
        arrived(z_over, half)
        spread(z_over, half)

    lane32 = iota((16, 128), 1) // 32
    seats = [jnp.where(lane32 == k, 1.0, 0.0).astype(bf16) for k in range(4)]

    def widen(quad):
        for b in range(PACK):
            base = pl.multiple_of((quad * PACK + b) * 16, 16)
            real, imag = turned[pl.ds(base, 8), :], turned[pl.ds(base + 8, 8), :]
            straight, crosswise = [], []
            for k in range(4):
                r = pltpu.roll(real, 32 * k, 1) if k else real
                i = pltpu.roll(imag, 32 * k, 1) if k else imag
                straight.append(jnp.concatenate([r, i], axis=0).astype(bf16))
                crosswise.append(jnp.concatenate([i, -r], axis=0).astype(bf16))
            seat = 2 * (b % PAIR)
            for p in range(4):
                tile = straight[(seat - p) % 4] * seats[seat] + crosswise[(seat + 1 - p) % 4] * seats[seat + 1]
                wide[quad * 2 + b // PAIR, pl.ds(p * 32 + (b % PAIR) * 16, 16), :] = tile

    loop(0, QUADS, widen)

    def result_out(first_row, count):
        rows = pl.ds(pl.multiple_of(first_row, S), count)
        return pltpu.make_async_copy(crossed.at[:, rows], crossed_hbm.at[:, rows], out_sem.at[1])

    def cross(block, half):
        for j in range(per_half):
            quad = place(block) * (2 * per_half) + half * per_half + j
            rows = pl.ds(pl.multiple_of(quad * S, S), S)
            for h in range(2):
                crossed[h, rows, :] = mxu(held[block, half * per_half + j, :, h * 128 : (h + 1) * 128], wide[quad * 2 + h])
        result_out((place(block) * 2 + half) * per_half * S, per_half * S).start()

    def near_block(half, step, zz):
        return at(y + step, zz, x) if half == 0 else at(y, zz, x + step)

    def far_block(half, step, along, zz):
        return at(along, zz, x + step) if half == 0 else at(y + step, zz, along)

    for zz in (z, z + 1):
        for half in (0, 1):
            for step in (-1, 1):
                block = near_block(half, step, zz)
                arrived(block, half)

                @pl.when(lax.rem(zz, NZ) == (0 if step == -1 else 1))
                def _():
                    hop(block, half, 1 if step == -1 else 2, first[half][0 if step == -1 else 1]).start()

                spread_last(block, half)

    for zz in (0, 1):
        for half in (0, 1):
            block = near_block(half, 2, zz)
            arrived(block, half)
            spread_last(block, half)

    for b in range(PACK):
        bins = slice(b * QUADS, (b + 1) * QUADS)
        fc, fs = far_cos[:, bins].T, far_sin[:, bins].T
        nc, ns = near_cos[bins, :], near_sin[bins, :]
        for a in range(LAGS // 128):
            columns = slice(a * 128, (a + 1) * 128)
            ca, sa = fc[:, a : a + 1], fs[:, a : a + 1]
            inverse[2 * b * QUADS : (2 * b + 1) * QUADS, columns] = (ca * nc - sa * ns).astype(bf16)
            inverse[(2 * b + 1) * QUADS : (2 * b + 2) * QUADS, columns] = -(sa * nc + ca * ns).astype(bf16)
    inverse_out = pltpu.make_async_copy(inverse, inverse_hbm, out_sem.at[0])
    inverse_out.start()

    def far_pass(i):
        yy, xx, zz = walk(i)
        for half in (0, 1):
            for step in (-1, 1):
                block = far_block(half, step, yy if half == 0 else xx, zz)
                arrived(block, half)

                @pl.when(zz == (0 if step == -1 else 1))
                def _():
                    hop(block, half, 3 if step == -1 else 4, last[half][0 if step == -1 else 1]).start()

                cross(block, half)

    loop(0, NY * NZ, far_pass)

    def cross_near(i):
        yy, xx, zz = walk(i)
        cross(at(yy, zz, x), 0)
        cross(at(y, zz, xx), 1)

    loop(0, NY * NZ, cross_near)

    def far_last(i):
        yy, xx, zz = walk(i)
        for half in (0, 1):
            block = far_block(half, 2, yy if half == 0 else xx, zz)
            arrived(block, half)
            cross(block, half)

    loop(0, NY * NZ, far_last)

    def finish_win(k):
        trade(k).wait_send()

    def finish_own(w):
        to_group(0, w, group, across).wait_send()
        to_group(1, w, group, sibling).wait_send()
        to_group(2, w, across, sibling).wait_send()

    def finish_halo(w):
        @pl.when(me < BLK - 1)
        def _():
            to_right(w).wait_send()

        @pl.when(me > 0)
        def _():
            to_left(w).wait_send()

    loop(1, WIN, finish_win)
    loop(0, 2 * tiles, finish_own)
    loop(1, BLK, lambda k: exchange(k).wait_send())
    loop(0, tiles, finish_halo)

    def sent(block, half, slot):
        hop(block, half, slot, z_over).wait_send()

    for half in (0, 1):
        sent(me, half, 0)
        for zz in (0, 1):
            for slot in (1, 2):
                sent(at(y, zz, x), half, slot)
        sent(near_block(half, -1, 0), half, 1)
        sent(near_block(half, 1, 1), half, 2)

    def sent_far(i):
        yy, xx, zz = walk(i)
        for half in (0, 1):
            block = at(yy, zz, x) if half == 0 else at(y, zz, xx)
            sent(block, half, 3)
            sent(block, half, 4)
            along = yy if half == 0 else xx

            @pl.when(zz == 0)
            def _():
                sent(far_block(half, -1, along, 0), half, 3)

            @pl.when(zz == 1)
            def _():
                sent(far_block(half, 1, along, 1), half, 4)

    loop(0, NY * NZ, sent_far)
    inverse_out.wait()
    result_out(0, QUADS * S).wait()


def to_lags(scaling, crossed, inverse, out, even, odd):
    def both(fill, full):
        out[...] = (mxu(full[...], inverse[...]) * scaling).reshape(8, C, LAGS)
        for s in range(8):
            for h in range(2):
                flipped = crossed[h, :, s, :].T.astype(bf16)
                for k in range(4):
                    columns = slice((h * 4 + k) * 128, (h * 4 + k + 1) * 128)
                    fill[s * C : (s + 1) * C, columns] = flipped[k * 32 : (k + 1) * 32]

    @pl.when(lax.rem(pl.program_id(0), 2) == 0)
    def _():
        both(even, odd)

    @pl.when(lax.rem(pl.program_id(0), 2) == 1)
    def _():
        both(odd, even)


def turn(bins, steps):
    phase = jnp.mod(bins * steps, L).astype(f32) * (2.0 * math.pi / L)
    return jnp.cos(phase), jnp.sin(phase)


def forward_parts():
    bins = (K0 + jnp.arange(F, dtype=i32))[None, :]
    return turn(bins, STEP * jnp.arange(L // STEP, dtype=i32)[:, None]) + turn(bins, jnp.arange(STEP, dtype=i32)[:, None])


def inverse_parts():
    bins = (K0 + PACK * jnp.arange(QUADS, dtype=i32)[None, :] + jnp.arange(PACK, dtype=i32)[:, None]).reshape(F)
    far = turn(bins[None, :], 128 * jnp.arange(LAGS // 128, dtype=i32)[:, None] - LAGS // 2)
    return far + turn(bins[:, None], jnp.arange(128, dtype=i32)[None, :])


def per_device(traces, filter_taps, good_channels, source_index):
    vmem = pl.BlockSpec(memory_space=pltpu.VMEM)
    smem = pl.BlockSpec(memory_space=pltpu.SMEM)
    anywhere = pl.BlockSpec(memory_space=pl.ANY)
    dma = pltpu.SemaphoreType.DMA
    crossed, inverse = pl.pallas_call(
        whole,
        out_shape=(
            jax.ShapeDtypeStruct((2, QUADS * S, 128), f32),
            jax.ShapeDtypeStruct((2 * F, LAGS), bf16),
        ),
        in_specs=[anywhere] + [vmem] * 11,
        out_specs=(anywhere, anywhere),
        scratch_shapes=[
            pltpu.VMEM((W * C, L), bf16),
            pltpu.VMEM((L, 256), bf16),
            pltpu.VMEM((F // 128, W, C, 256), f32),
            pltpu.VMEM((F // 128, W, HALO, 256), f32),
            pltpu.VMEM((F // 128, W, HALO, 256), f32),
            pltpu.VMEM((F // 128, W * C, 256), f32),
            pltpu.VMEM((3 * W * C, F + 256), bf16),
            pltpu.VMEM((BLK, C, 2 * W * BINS), bf16),
            pltpu.VMEM((BLK, C, 2 * W * BINS), bf16),
            pltpu.VMEM((WIN, S, 2 * W * BINS), bf16),
            pltpu.VMEM((WIN, S, 2 * W * BINS), bf16),
            pltpu.VMEM((WIN, 2 * F // 128, W * C, 128), bf16),
            pltpu.VMEM((BINS // PACK, S, 256), bf16),
            pltpu.VMEM((BLK, BINS // PACK, S, 256), bf16),
            pltpu.VMEM((F * 16, 128), f32),
            pltpu.VMEM((QUADS * 2, 128, 128), bf16),
            pltpu.VMEM((2, QUADS * S, 128), f32),
            pltpu.VMEM((2 * F, LAGS), bf16),
            dma((2, F // 128)), dma((2, F // 128)), dma((BLK,)), dma((BLK,)),
            dma((3, 2 * F // 128)), dma((3, 2 * F // 128)), dma((WIN,)), dma((WIN,)),
            dma((BLK, 2, 5)), dma((BLK, 2)), dma((3,)),
        ],
        compiler_params=pltpu.CompilerParams(
            collective_id=0, has_side_effects=True, vmem_limit_bytes=60 << 20
        ),
        name="whole",
    )(
        traces.reshape(W * C, L), good_channels.astype(i32)[None, :], filter_taps[None, :],
        source_index.astype(i32)[None, :], *forward_parts(), *inverse_parts(),
    )

    return pl.pallas_call(
        functools.partial(to_lags, 1.0 / math.sqrt(F * W * WIN)),
        grid=(S // 8 + 1,),
        out_shape=jax.ShapeDtypeStruct((S, C, LAGS), f32),
        in_specs=[
            pl.BlockSpec((2, QUADS, 8, 128), lambda i: (0, 0, jnp.minimum(i, S // 8 - 1), 0)),
            pl.BlockSpec((2 * F, LAGS), lambda i: (0, 0), pipeline_mode=pl.Buffered(1)),
        ],
        out_specs=pl.BlockSpec((8, C, LAGS), lambda i: (jnp.maximum(i - 1, 0), 0, 0)),
        scratch_shapes=[pltpu.VMEM((8 * C, 2 * F), bf16)] * 2,
        compiler_params=pltpu.CompilerParams(vmem_limit_bytes=62 << 20),
        name="to_lags",
    )(crossed.reshape(2, QUADS, S, 128), inverse)


def solution(mesh):
    placed = (P("win", "chan", None), P(), P("chan"), P())
    return jax.shard_map(
        per_device, mesh=mesh, in_specs=placed, out_specs=P("win", "chan", None), check_vma=False
    )
```

```python
import math

import jax
import jax.numpy as jnp
from jax import lax
from jax.experimental import pallas as pl
from jax.experimental.pallas import tpu as pltpu
from jax.sharding import PartitionSpec as P

L = 7680
F = 512
LAGS = 2048
HALO = 16
SMOOTH = 64
K0 = 31

WIN = 4
BLK = 32
NX = 4
NZ = 2
NY = 4
W = 8
C = 32
S = 64
BINS = F // BLK
QUADS = F // 4
PACK = 4
PAIR = 2
LIMIT = 54
STEP = 64
DEEP = 2 * W * WIN
MESH = pl.DeviceIdType.MESH
f32, bf16, i32 = jnp.float32, jnp.bfloat16, jnp.int32


def iota(shape, dim):
    return lax.broadcasted_iota(i32, shape, dim)


def mxu(a, b):
    return jnp.dot(a, b, preferred_element_type=f32)


def loop(start, stop, body):
    def step(i, carry):
        body(i)
        return carry

    lax.fori_loop(start, stop, step, 0)


def thirds(x):
    high = x.astype(bf16)
    rest = x - high.astype(f32)
    middle = rest.astype(bf16)
    low = (rest - middle.astype(f32)).astype(bf16)
    return high, middle, low


def chan_copy(src, dst, send, recv, peer):
    return pltpu.make_async_remote_copy(
        src_ref=src, dst_ref=dst, send_sem=send, recv_sem=recv,
        device_id=(lax.axis_index("win"), peer), device_id_type=MESH,
    )


def win_copy(src, dst, send, recv, peer):
    return pltpu.make_async_remote_copy(
        src_ref=src, dst_ref=dst, send_sem=send, recv_sem=recv,
        device_id=(peer, lax.axis_index("chan")), device_id_type=MESH,
    )


def diagonal(row, count):
    return jnp.sum(jnp.where(iota((count, count), 0) == iota((count, count), 1), row, 0.0), axis=1, keepdims=True)


def whole(
    traces, good, taps, sources, cosines, sines, stacked_out, inverse_out,
    row_cos, row_sin, step_cos, step_sin, near_cos, near_sin, far, spread_pair, stacked, rows, table, spec, low, high, filtered, magnitudes, outgoing, mixed, chosen, regroup, own, quads, held, turned, wide,
    crossed, inverse,
    halo_send, halo_recv, all_send, all_recv, own_send, own_recv, win_send, win_recv, send, recv, out_sem,
):
    me = lax.axis_index("chan")
    group = lax.axis_index("win")
    y, z, x = me // (NZ * NX), lax.rem(me // NX, NZ), lax.rem(me, NX)
    layer, core = group // 2, lax.rem(group, 2)
    sibling, across, diagonal_group = layer * 2 + 1 - core, (1 - layer) * 2 + core, (1 - layer) * 2 + 1 - core

    rows_in = pltpu.make_async_copy(traces, rows, out_sem.at[2])
    rows_in.start()
    barrier = pltpu.get_barrier_semaphore()

    def greet_chan(k):
        pl.semaphore_signal(barrier, inc=1, device_id=(group, lax.rem(me + k, BLK)), device_id_type=MESH)

    def greet_win(k):
        pl.semaphore_signal(barrier, inc=1, device_id=(lax.rem(group + k, WIN), me), device_id_type=MESH)

    loop(1, BLK, greet_chan)
    loop(1, WIN, greet_win)

    offset = iota((C, C + 2 * HALO), 1) - iota((C, C + 2 * HALO), 0)
    weights = taps[...].astype(f32)
    band = jnp.where(offset == HALO, 1.0, 0.0)
    for o in range(HALO):
        band = jnp.where(offset == o, -weights[:, o : o + 1], band)
        band = jnp.where(offset == HALO + 1 + o, -weights[:, HALO + o : HALO + o + 1], band)
    band = jnp.concatenate([band, band, band], axis=1).astype(bf16)
    keep = diagonal(good[...].astype(f32), C)
    beside = jnp.where(jnp.abs(iota((384, 128), 0) - 128 - iota((384, 128), 1)) <= SMOOTH, 1.0, 0.0).astype(bf16)
    magnitudes[:, 0:128] = jnp.zeros((3 * W * C, 128), bf16)
    magnitudes[:, 640:768] = jnp.zeros((3 * W * C, 128), bf16)

    @pl.when(me == 0)
    def _():
        low[...] = jnp.zeros_like(low)

    @pl.when(me == BLK - 1)
    def _():
        high[...] = jnp.zeros_like(high)

    def sums(a, b):
        ca, sa, cb, sb = cosines[a, :], sines[a, :], cosines[b, :], sines[b, :]
        return ca * cb - sa * sb, sa * cb + ca * sb

    for i in range(L // STEP // 8):
        row_cos[i * 8 : (i + 1) * 8, :], row_sin[i * 8 : (i + 1) * 8, :] = sums(slice(i, i + 1), slice(16, 24))
    for i in range(STEP // 8):
        step_cos[i * 8 : (i + 1) * 8, :], step_sin[i * 8 : (i + 1) * 8, :] = sums(slice(24 + i, 25 + i), slice(32, 40))

    tiles = F // 128
    per_tile = 128 // BINS
    right, left = lax.rem(me + 1, BLK), lax.rem(me + BLK - 1, BLK)

    def to_right(n):
        return chan_copy(spec.at[n, :, pl.ds(C - HALO, HALO)], low.at[n], halo_send.at[0, n], halo_recv.at[0, n], right)

    def to_left(n):
        return chan_copy(spec.at[n, :, pl.ds(0, HALO)], high.at[n], halo_send.at[1, n], halo_recv.at[1, n], left)

    def tile_of(n):
        return pl.ds(pl.multiple_of(n * 128, 128), 128)

    def transform(n):
        columns = tile_of(n)
        cb, sb = step_cos[:, columns], step_sin[:, columns]

        def table_rows(i):
            eight = pl.ds(pl.multiple_of(i * 8, 8), 8)
            cas, sas = row_cos[eight, columns], row_sin[eight, columns]
            for u in range(8):
                ca, sa = cas[u : u + 1], sas[u : u + 1]
                at_rows = pl.ds(pl.multiple_of((i * 8 + u) * STEP, STEP), STEP)
                table[at_rows, 0:128] = (ca * cb - sa * sb).astype(bf16)
                table[at_rows, 128:256] = (-sa * cb - ca * sb).astype(bf16)

        loop(0, L // STEP // 8, table_rows)

        @pl.when(n == 0)
        def _():
            rows_in.wait()

        spec[n] = mxu(rows[...], table[...]).reshape(W, C, 256) * keep

        @pl.when(n == 0)
        def _():
            pl.semaphore_wait(barrier, BLK + WIN - 2)

        @pl.when(me < BLK - 1)
        def _():
            to_right(n).start()

        @pl.when(me > 0)
        def _():
            to_left(n).start()

    def filter_tile(n):
        @pl.when(me > 0)
        def _():
            to_right(n).wait_recv()

        @pl.when(me < BLK - 1)
        def _():
            to_left(n).wait_recv()

        for w in range(W):
            padded = jnp.concatenate([low[n, w], spec[n, w], high[n, w]], axis=0)
            out = mxu(band, jnp.concatenate(thirds(padded), axis=0)) * keep
            filtered[n, w * C : (w + 1) * C, :] = out
            real, imag = out[:, :128], out[:, 128:]
            for k, part in enumerate(thirds(jnp.sqrt(real * real + imag * imag))):
                magnitudes[(k * W + w) * C : (k * W + w + 1) * C, tile_of(n + 1)] = part

    lane = iota((C, 128), 1) // BINS

    def exchange(k):
        peer = lax.rem(me + k, BLK)
        return chan_copy(outgoing.at[peer], mixed.at[me], all_send.at[k], all_recv.at[k], peer)

    def to_group(hop, tile, whose, peer):
        return win_copy(own.at[whose, tile], own.at[whose, tile], own_send.at[hop, tile], own_recv.at[hop, tile], peer)

    def turn_tile(whose, part, tile):
        for half in range(2):
            block = own[whose, part * tiles + tile, half * 128 : (half + 1) * 128, :]
            start = part * F * 8 + tile * 128 * 8 + whose * 2 + half
            turned[pl.ds(start, 128, stride=8), :] = block.astype(f32).T

    def turn_group(whose):
        def both(tile):
            turn_tile(whose, 0, tile)
            turn_tile(whose, 1, tile)

        loop(0, tiles, both)

    def home(n, m):
        return (m // NZ) * NZ * NX + (m % NZ) * NX + lax.rem(n + m // NZ, NX)

    def place(block):
        yy, zz, xx = block // (NZ * NX), lax.rem(block // NX, NZ), lax.rem(block, NX)
        return lax.rem(xx - yy + NX, NX) * per_tile + yy * NZ + zz

    def whiten_tile(n):
        sums = mxu(magnitudes[:, pl.ds(pl.multiple_of(n * 128, 128), 384)], beside)
        bins = iota((1, 128), 1) + n * 128
        count = 1 + jnp.minimum(bins, SMOOTH) + jnp.minimum(F - 1 - bins, SMOOTH)
        total = sums[: W * C] + sums[W * C : 2 * W * C] + sums[2 * W * C :]
        inverse_amplitude = 1.0 / (total * (1.0 / count.astype(f32)) + 1e-06)
        for part in range(2):
            values = filtered[n, :, part * 128 : (part + 1) * 128] * inverse_amplitude
            own[group, part * tiles + n] = values.astype(bf16)
            windows = [values[w * C : (w + 1) * C] for w in range(W)]
            for d in (1, 2, 4):
                clear = lane // d % 2 == 0
                before = list(windows)
                for w in range(W):
                    if not w & d:
                        a, b = before[w], before[w | d]
                        windows[w] = jnp.where(clear, a, pltpu.roll(b, d * BINS, 1))
                        windows[w | d] = jnp.where(clear, pltpu.roll(a, 128 - d * BINS, 1), b)
            for m in range(per_tile):
                outgoing[home(n, m), :, part * 128 : (part + 1) * 128] = windows[m].astype(bf16)
        for m in range(per_tile):
            peer = home(n, m)

            @pl.when(peer != me)
            def _():
                exchange(lax.rem(peer - me + BLK, BLK)).start()

        for part in range(2):
            to_group(0, part * tiles + n, group, across).start()
            to_group(1, part * tiles + n, group, sibling).start()

    def stage(n):
        @pl.when(n < tiles)
        def _():
            transform(n)

        @pl.when((n >= 2) & (n < tiles + 2))
        def _():
            filter_tile(n - 2)

        @pl.when(n >= 3)
        def _():
            whiten_tile(n - 3)

    loop(0, tiles + 3, stage)
    mixed[me] = outgoing[me]

    wanted = jnp.where(iota((WIN * S, BLK * C), 1) == diagonal(sources[...].astype(f32), WIN * S).astype(i32), 1.0, 0.0).astype(bf16)
    span = 2 * W * BINS
    source = iota((span, 1), 0)
    window, one = lax.rem(source // BINS, W), lax.rem(source, BINS)
    pair, seat = one // PACK * 2 + lax.rem(one, 2), lax.rem(one // 2, 2)
    target = pair * 128 + lax.rem(window, 4) * 32 + seat * 16 + source // (W * BINS) * 8 + window // 4
    order = jnp.where(iota((span, WIN * span), 1) == target, 1.0, 0.0).astype(bf16)
    column = iota((1, 1024), 1)
    kind, part = lax.rem(column // 128, 2), lax.rem(column // 32, 2)
    origin = jnp.where(kind == part, 0, 128) + column // 256 * 32 + lax.rem(column, 32)
    sign = jnp.where(kind * part == 1, -1.0, 1.0)
    for b in range(PAIR):
        used = jnp.where(lax.rem(column // 64, 2) == b, origin, -1)
        spread_pair[b] = jnp.where(iota((256, 1024), 0) == used, sign, 0.0).astype(bf16)
    turn_group(group)
    loop(0, 2 * tiles, lambda t: to_group(1, t, sibling, sibling).wait_recv())
    turn_group(sibling)

    loop(1, BLK, lambda k: exchange(k).wait_recv())
    picked = mxu(wanted, mixed[...].reshape(BLK * C, 2 * W * BINS)).astype(bf16)
    chosen[...] = picked.reshape(WIN, S, 2 * W * BINS)

    def trade(k):
        peer = lax.rem(group + k, WIN)
        return win_copy(chosen.at[peer], regroup.at[group], win_send.at[k], win_recv.at[k], peer)

    loop(1, WIN, lambda k: trade(k).start())
    regroup[group] = chosen[group]

    def relay(t):
        to_group(0, t, across, across).wait_recv()
        to_group(2, t, across, sibling).start()

    loop(0, 2 * tiles, relay)
    turn_group(across)
    loop(1, WIN, lambda k: trade(k).wait_recv())
    arranged = mxu(regroup[0], order)
    for g in range(1, WIN):
        arranged += pltpu.roll(mxu(regroup[g], order), 2 * g, 1)
    for q in range(BINS // PACK):
        quads[q] = arranged[:, q * 256 : (q + 1) * 256].astype(bf16)

    def at(yy, zz, xx):
        return (lax.rem(yy + NY, NY) * NZ + lax.rem(zz, NZ)) * NX + lax.rem(xx + NX, NX)

    y_up, y_down, x_up, x_down, z_over = at(y + 1, z, x), at(y - 1, z, x), at(y, z, x + 1), at(y, z, x - 1), at(y, z + 1, x)

    first = ((y_up, y_down), (x_up, x_down))
    last = ((x_up, x_down), (y_up, y_down))
    per_half = BINS // PACK // 2

    def piece(block, half):
        return held.at[block, pl.ds(half * per_half, per_half)]

    def hop(block, half, slot, peer, src=None):
        src = piece(block, half) if src is None else src
        return chan_copy(src, piece(block, half), send.at[block, half, slot], recv.at[block, half], peer)

    def own_piece(half):
        return quads.at[pl.ds(half * per_half, per_half)]

    def arrived(block, half):
        hop(block, half, 0, z_over).wait_recv()

    def spread_last(block, half, src=None):
        hop(block, half, 3, last[half][0], src).start()
        hop(block, half, 4, last[half][1], src).start()

    def spread(block, half, src=None):
        hop(block, half, 1, first[half][0], src).start()
        hop(block, half, 2, first[half][1], src).start()
        spread_last(block, half, src)

    def walk(i):
        k = i // NZ
        k = jnp.where(k > 1, 5 - k, k)
        return lax.rem(y + k, NY), lax.rem(x + k, NX), lax.rem(i, NZ)

    for half in (0, 1):
        hop(me, half, 0, z_over, own_piece(half)).start()
    for half in (0, 1):
        spread(me, half, own_piece(half))
    for q in range(2 * per_half):
        held[me, q] = quads[q]

    loop(0, 2 * tiles, lambda t: to_group(2, t, diagonal_group, sibling).wait_recv())
    turn_group(diagonal_group)

    for half in (0, 1):
        arrived(z_over, half)
        spread(z_over, half)

    def widen(i):
        start = pl.multiple_of(i * 512, 512)
        real, imag = turned[pl.ds(start, 512), :], turned[pl.ds(F * 8 + start, 512), :]
        both = jnp.concatenate([real, imag], axis=1).reshape(16, 2, 16, 256)
        for b in range(PAIR):
            spread_rows = mxu(both[:, b].reshape(256, 256).astype(bf16), spread_pair[b])
            for p in range(4):
                upper = spread_rows[:, p * 256 : p * 256 + 128].reshape(32, 8, 128)
                lower = spread_rows[:, p * 256 + 128 : p * 256 + 256].reshape(32, 8, 128)
                tile = jnp.concatenate([upper, lower], axis=1).astype(bf16)
                wide[pl.ds(pl.multiple_of(i * 32, 32), 32), p * 32 + b * 16 : p * 32 + b * 16 + 16, :] = tile

    loop(0, F * 8 // 512, widen)

    def cross(block, half):
        for j in range(per_half):
            quad = place(block) * (2 * per_half) + half * per_half + j
            rows = pl.ds(pl.multiple_of(quad * S, S), S)
            for h in range(2):
                crossed[h, rows, :] = mxu(held[block, half * per_half + j, :, h * 128 : (h + 1) * 128], wide[quad * 2 + h])

    def near_block(half, step, zz):
        return at(y + step, zz, x) if half == 0 else at(y, zz, x + step)

    def far_block(half, step, along, zz):
        return at(along, zz, x + step) if half == 0 else at(y + step, zz, along)

    for zz in (z, z + 1):
        for half in (0, 1):
            for step in (-1, 1):
                block = near_block(half, step, zz)
                arrived(block, half)

                @pl.when(lax.rem(zz, NZ) == (0 if step == -1 else 1))
                def _():
                    hop(block, half, 1 if step == -1 else 2, first[half][0 if step == -1 else 1]).start()

                spread_last(block, half)

    for zz in (0, 1):
        for half in (0, 1):
            block = near_block(half, 2, zz)
            arrived(block, half)
            spread_last(block, half)

    ca, sa, cb, sb = row_cos[1:2, :], row_sin[1:2, :], step_cos[...], step_sin[...]
    near_cos[...] = jnp.concatenate([cb, ca * cb - sa * sb], axis=0).T
    near_sin[...] = jnp.concatenate([sb, sa * cb + ca * sb], axis=0).T
    lags = [128 // STEP * a - LAGS // 2 // STEP for a in range(LAGS // 128)]
    angles = [row_cos[abs(a) : abs(a) + 1, :] for a in lags]
    angles += [row_sin[abs(a) : abs(a) + 1, :] * (1.0 if a >= 0 else -1.0) for a in lags]
    far[...] = jnp.concatenate(angles + [jnp.zeros((128 - len(angles), F), f32)], axis=0).T
    for b in range(PAIR):
        for h in range(2):
            bins = pl.ds(2 * b + h, QUADS, stride=PACK)
            nc, ns, fc = near_cos[bins, :], near_sin[bins, :], far[bins, :]
            k = (h * 4 + b * 2) * QUADS
            for a in range(LAGS // 128):
                columns = slice(a * 128, (a + 1) * 128)
                ca, sa = fc[:, a : a + 1], fc[:, len(lags) + a : len(lags) + a + 1]
                inverse[k : k + QUADS, columns] = (ca * nc - sa * ns).astype(bf16)
                inverse[k + QUADS : k + 2 * QUADS, columns] = (-sa * nc - ca * ns).astype(bf16)
    inverse_copy = pltpu.make_async_copy(inverse, inverse_out, out_sem.at[0])
    inverse_copy.start()

    def far_pass(i):
        yy, xx, zz = walk(i)
        for half in (0, 1):
            for step in (-1, 1):
                block = far_block(half, step, yy if half == 0 else xx, zz)
                arrived(block, half)

                @pl.when(zz == (0 if step == -1 else 1))
                def _():
                    hop(block, half, 3 if step == -1 else 4, last[half][0 if step == -1 else 1]).start()

                cross(block, half)

    loop(0, NY * NZ, far_pass)

    def cross_near(i):
        yy, xx, zz = walk(i)
        cross(at(yy, zz, x), 0)
        cross(at(y, zz, xx), 1)

    loop(0, NY * NZ, cross_near)

    def far_last(i):
        yy, xx, zz = walk(i)
        for half in (0, 1):
            block = far_block(half, 2, yy if half == 0 else xx, zz)
            arrived(block, half)
            cross(block, half)

    loop(0, NY * NZ, far_last)

    def stacked_copy(first, count):
        where = pl.ds(pl.multiple_of(first, 8 * C), count)
        return pltpu.make_async_copy(stacked.at[where], stacked_out.at[where], out_sem.at[1])

    def turn_sources(i):
        for u in range(8):
            where = pl.ds(pl.multiple_of((i * 8 + u) * C, C), C)
            for h in range(2):
                flipped = crossed[h, pl.ds(i * 8 + u, QUADS, stride=S), :].T.astype(bf16)
                for k in range(4):
                    stacked[where, (h * 4 + k) * 128 : (h * 4 + k + 1) * 128] = flipped[k * 32 : (k + 1) * 32]
        stacked_copy(i * 8 * C, 8 * C).start()

    loop(0, S // 8, turn_sources)

    def finish_win(k):
        trade(k).wait_send()

    def finish_own(w):
        to_group(0, w, group, across).wait_send()
        to_group(1, w, group, sibling).wait_send()
        to_group(2, w, across, sibling).wait_send()

    def finish_halo(w):
        @pl.when(me < BLK - 1)
        def _():
            to_right(w).wait_send()

        @pl.when(me > 0)
        def _():
            to_left(w).wait_send()

    loop(1, WIN, finish_win)
    loop(0, 2 * tiles, finish_own)
    loop(1, BLK, lambda k: exchange(k).wait_send())
    loop(0, tiles, finish_halo)

    def sent(block, half, slot):
        hop(block, half, slot, z_over).wait_send()

    for half in (0, 1):
        sent(me, half, 0)
        for zz in (0, 1):
            for slot in (1, 2):
                sent(at(y, zz, x), half, slot)
        sent(near_block(half, -1, 0), half, 1)
        sent(near_block(half, 1, 1), half, 2)

    def sent_far(i):
        yy, xx, zz = walk(i)
        for half in (0, 1):
            block = at(yy, zz, x) if half == 0 else at(y, zz, xx)
            sent(block, half, 3)
            sent(block, half, 4)
            along = yy if half == 0 else xx

            @pl.when(zz == 0)
            def _():
                sent(far_block(half, -1, along, 0), half, 3)

            @pl.when(zz == 1)
            def _():
                sent(far_block(half, 1, along, 1), half, 4)

    loop(0, NY * NZ, sent_far)
    inverse_copy.wait()
    stacked_copy(0, S * C).wait()


def turn(bins, steps):
    phase = jnp.mod(bins * steps, L).astype(f32) * (2.0 * math.pi / L)
    return jnp.cos(phase), jnp.sin(phase)


def angle_parts():
    count = jnp.arange(40, dtype=i32)
    scale = jnp.where(count < 16, 8 * STEP, jnp.where(count < 24, STEP, jnp.where(count < 32, 8, 1)))
    steps = jnp.where(count < 16, count, count % 8) * scale
    return turn((K0 + jnp.arange(F, dtype=i32))[None, :], steps[:, None])


def per_device(traces, filter_taps, good_channels, source_index):
    vmem = pl.BlockSpec(memory_space=pltpu.VMEM)
    smem = pl.BlockSpec(memory_space=pltpu.SMEM)
    anywhere = pl.BlockSpec(memory_space=pl.ANY)
    dma = pltpu.SemaphoreType.DMA
    stacked, inverse = pl.pallas_call(
        whole,
        out_shape=(
            jax.ShapeDtypeStruct((S * C, 2 * F), bf16),
            jax.ShapeDtypeStruct((2 * F, LAGS), bf16),
        ),
        in_specs=[anywhere] + [vmem] * 5,
        out_specs=(anywhere, anywhere),
        scratch_shapes=[
            pltpu.VMEM((L // STEP, F), f32),
            pltpu.VMEM((L // STEP, F), f32),
            pltpu.VMEM((STEP, F), f32),
            pltpu.VMEM((STEP, F), f32),
            pltpu.VMEM((F, 128), f32),
            pltpu.VMEM((F, 128), f32),
            pltpu.VMEM((F, 128), f32),
            pltpu.VMEM((PAIR, 256, 1024), bf16),
            pltpu.VMEM((S * C, 2 * F), bf16),
            pltpu.VMEM((W * C, L), bf16),
            pltpu.VMEM((L, 256), bf16),
            pltpu.VMEM((F // 128, W, C, 256), f32),
            pltpu.VMEM((F // 128, W, HALO, 256), f32),
            pltpu.VMEM((F // 128, W, HALO, 256), f32),
            pltpu.VMEM((F // 128, W * C, 256), f32),
            pltpu.VMEM((3 * W * C, F + 256), bf16),
            pltpu.VMEM((BLK, C, 2 * W * BINS), bf16),
            pltpu.VMEM((BLK, C, 2 * W * BINS), bf16),
            pltpu.VMEM((WIN, S, 2 * W * BINS), bf16),
            pltpu.VMEM((WIN, S, 2 * W * BINS), bf16),
            pltpu.VMEM((WIN, 2 * F // 128, W * C, 128), bf16),
            pltpu.VMEM((BINS // PACK, S, 256), bf16),
            pltpu.VMEM((BLK, BINS // PACK, S, 256), bf16),
            pltpu.VMEM((F * 16, 128), f32),
            pltpu.VMEM((QUADS * 2, 128, 128), bf16),
            pltpu.VMEM((2, QUADS * S, 128), f32),
            pltpu.VMEM((2 * F, LAGS), bf16),
            dma((2, F // 128)), dma((2, F // 128)), dma((BLK,)), dma((BLK,)),
            dma((3, 2 * F // 128)), dma((3, 2 * F // 128)), dma((WIN,)), dma((WIN,)),
            dma((BLK, 2, 5)), dma((BLK, 2)), dma((3,)),
        ],
        compiler_params=pltpu.CompilerParams(
            collective_id=0, has_side_effects=True, vmem_limit_bytes=LIMIT << 20
        ),
        name="whole",
    )(
        traces.reshape(W * C, L), good_channels.astype(i32)[None, :], filter_taps[None, :],
        source_index.astype(i32)[None, :], *angle_parts(),
    )

    scaling = 1.0 / math.sqrt(F * W * WIN)
    return (mxu(stacked, inverse) * scaling).reshape(S, C, LAGS)


def solution(mesh):
    placed = (P("win", "chan", None), P(), P("chan"), P())
    return jax.shard_map(
        per_device, mesh=mesh, in_specs=placed, out_specs=P("win", "chan", None), check_vma=False
    )
```

```python
import functools
import math

import jax
import jax.numpy as jnp
from jax import lax
from jax.experimental import pallas as pl
from jax.experimental.pallas import tpu as pltpu
from jax.sharding import PartitionSpec as P

L = 7680
F = 512
LAGS = 2048
HALO = 16
SMOOTH = 64
K0 = 31

WIN = 4
BLK = 32
NX = 4
NZ = 2
NY = 4
W = 8
C = 32
S = 64
BINS = F // BLK
QUADS = F // 4
PACK = 4
PAIR = 2
LIMIT = 54
AT_ONCE = 16
STEP = 64
DEEP = 2 * W * WIN
MESH = pl.DeviceIdType.MESH
f32, bf16, i32 = jnp.float32, jnp.bfloat16, jnp.int32


def iota(shape, dim):
    return lax.broadcasted_iota(i32, shape, dim)


def mxu(a, b):
    return jnp.dot(a, b, preferred_element_type=f32)


def loop(start, stop, body):
    def step(i, carry):
        body(i)
        return carry

    lax.fori_loop(start, stop, step, 0)


def thirds(x):
    high = x.astype(bf16)
    rest = x - high.astype(f32)
    middle = rest.astype(bf16)
    low = (rest - middle.astype(f32)).astype(bf16)
    return high, middle, low


def chan_copy(src, dst, send, recv, peer):
    return pltpu.make_async_remote_copy(
        src_ref=src, dst_ref=dst, send_sem=send, recv_sem=recv,
        device_id=(lax.axis_index("win"), peer), device_id_type=MESH,
    )


def win_copy(src, dst, send, recv, peer):
    return pltpu.make_async_remote_copy(
        src_ref=src, dst_ref=dst, send_sem=send, recv_sem=recv,
        device_id=(peer, lax.axis_index("chan")), device_id_type=MESH,
    )


def diagonal(row, count):
    return jnp.sum(jnp.where(iota((count, count), 0) == iota((count, count), 1), row, 0.0), axis=1, keepdims=True)


def whole(
    traces, good, taps, sources, cosines, sines, stacked_out, inverse_out,
    row_cos, row_sin, step_cos, step_sin, near_cos, near_sin, far, spread_pair, stacked, rows, table, spec, low, high, filtered, magnitudes, outgoing, mixed, chosen, regroup, own, quads, held, turned, wide,
    crossed, inverse,
    halo_send, halo_recv, all_send, all_recv, own_send, own_recv, win_send, win_recv, send, recv, out_sem,
):
    me = lax.axis_index("chan")
    group = lax.axis_index("win")
    y, z, x = me // (NZ * NX), lax.rem(me // NX, NZ), lax.rem(me, NX)
    layer, core = group // 2, lax.rem(group, 2)
    sibling, across, diagonal_group = layer * 2 + 1 - core, (1 - layer) * 2 + core, (1 - layer) * 2 + 1 - core

    rows_in = pltpu.make_async_copy(traces, rows, out_sem.at[2])
    rows_in.start()
    barrier = pltpu.get_barrier_semaphore()

    def greet_chan(k):
        pl.semaphore_signal(barrier, inc=1, device_id=(group, lax.rem(me + k, BLK)), device_id_type=MESH)

    def greet_win(k):
        pl.semaphore_signal(barrier, inc=1, device_id=(lax.rem(group + k, WIN), me), device_id_type=MESH)

    loop(1, BLK, greet_chan)
    loop(1, WIN, greet_win)

    offset = iota((C, C + 2 * HALO), 1) - iota((C, C + 2 * HALO), 0)
    weights = taps[...].astype(f32)
    band = jnp.where(offset == HALO, 1.0, 0.0)
    for o in range(HALO):
        band = jnp.where(offset == o, -weights[:, o : o + 1], band)
        band = jnp.where(offset == HALO + 1 + o, -weights[:, HALO + o : HALO + o + 1], band)
    band = jnp.concatenate([band, band, band], axis=1).astype(bf16)
    keep = diagonal(good[...].astype(f32), C)
    beside = jnp.where(jnp.abs(iota((384, 128), 0) - 128 - iota((384, 128), 1)) <= SMOOTH, 1.0, 0.0).astype(bf16)
    magnitudes[:, 0:128] = jnp.zeros((3 * W * C, 128), bf16)
    magnitudes[:, 640:768] = jnp.zeros((3 * W * C, 128), bf16)

    @pl.when(me == 0)
    def _():
        low[...] = jnp.zeros_like(low)

    @pl.when(me == BLK - 1)
    def _():
        high[...] = jnp.zeros_like(high)

    def sums(a, b):
        ca, sa, cb, sb = cosines[a, :], sines[a, :], cosines[b, :], sines[b, :]
        return ca * cb - sa * sb, sa * cb + ca * sb

    for i in range(L // STEP // 8):
        row_cos[i * 8 : (i + 1) * 8, :], row_sin[i * 8 : (i + 1) * 8, :] = sums(slice(i, i + 1), slice(16, 24))
    for i in range(STEP // 8):
        step_cos[i * 8 : (i + 1) * 8, :], step_sin[i * 8 : (i + 1) * 8, :] = sums(slice(24 + i, 25 + i), slice(32, 40))

    tiles = F // 128
    per_tile = 128 // BINS
    right, left = lax.rem(me + 1, BLK), lax.rem(me + BLK - 1, BLK)

    def to_right(n):
        return chan_copy(spec.at[n, :, pl.ds(C - HALO, HALO)], low.at[n], halo_send.at[0, n], halo_recv.at[0, n], right)

    def to_left(n):
        return chan_copy(spec.at[n, :, pl.ds(0, HALO)], high.at[n], halo_send.at[1, n], halo_recv.at[1, n], left)

    def tile_of(n):
        return pl.ds(pl.multiple_of(n * 128, 128), 128)

    def transform(n):
        columns = tile_of(n)
        cb, sb = step_cos[:, columns], step_sin[:, columns]

        def table_rows(i):
            eight = pl.ds(pl.multiple_of(i * 8, 8), 8)
            cas, sas = row_cos[eight, columns], row_sin[eight, columns]
            for u in range(8):
                ca, sa = cas[u : u + 1], sas[u : u + 1]
                at_rows = pl.ds(pl.multiple_of((i * 8 + u) * STEP, STEP), STEP)
                table[at_rows, 0:128] = (ca * cb - sa * sb).astype(bf16)
                table[at_rows, 128:256] = (-sa * cb - ca * sb).astype(bf16)

        loop(0, L // STEP // 8, table_rows)

        @pl.when(n == 0)
        def _():
            rows_in.wait()

        spec[n] = mxu(rows[...], table[...]).reshape(W, C, 256) * keep

        @pl.when(n == 0)
        def _():
            pl.semaphore_wait(barrier, BLK + WIN - 2)

        @pl.when(me < BLK - 1)
        def _():
            to_right(n).start()

        @pl.when(me > 0)
        def _():
            to_left(n).start()

    def filter_tile(n):
        @pl.when(me > 0)
        def _():
            to_right(n).wait_recv()

        @pl.when(me < BLK - 1)
        def _():
            to_left(n).wait_recv()

        for w in range(W):
            padded = jnp.concatenate([low[n, w], spec[n, w], high[n, w]], axis=0)
            out = mxu(band, jnp.concatenate(thirds(padded), axis=0)) * keep
            filtered[n, w * C : (w + 1) * C, :] = out
            real, imag = out[:, :128], out[:, 128:]
            for k, part in enumerate(thirds(jnp.sqrt(real * real + imag * imag))):
                magnitudes[(k * W + w) * C : (k * W + w + 1) * C, tile_of(n + 1)] = part

    lane = iota((C, 128), 1) // BINS

    def exchange(k):
        peer = lax.rem(me + k, BLK)
        return chan_copy(outgoing.at[peer], mixed.at[me], all_send.at[k], all_recv.at[k], peer)

    def to_group(hop, tile, whose, peer):
        return win_copy(own.at[whose, tile], own.at[whose, tile], own_send.at[hop, tile], own_recv.at[hop, tile], peer)

    def turn_tile(whose, part, tile):
        for half in range(2):
            block = own[whose, part * tiles + tile, half * 128 : (half + 1) * 128, :]
            start = part * F * 8 + tile * 128 * 8 + whose * 2 + half
            turned[pl.ds(start, 128, stride=8), :] = block.astype(f32).T

    def turn_group(whose):
        def both(tile):
            turn_tile(whose, 0, tile)
            turn_tile(whose, 1, tile)

        loop(0, tiles, both)

    def home(n, m):
        return (m // NZ) * NZ * NX + (m % NZ) * NX + lax.rem(n + m // NZ, NX)

    def place(block):
        yy, zz, xx = block // (NZ * NX), lax.rem(block // NX, NZ), lax.rem(block, NX)
        return lax.rem(xx - yy + NX, NX) * per_tile + yy * NZ + zz

    def whiten_tile(n):
        sums = mxu(magnitudes[:, pl.ds(pl.multiple_of(n * 128, 128), 384)], beside)
        bins = iota((1, 128), 1) + n * 128
        count = 1 + jnp.minimum(bins, SMOOTH) + jnp.minimum(F - 1 - bins, SMOOTH)
        total = sums[: W * C] + sums[W * C : 2 * W * C] + sums[2 * W * C :]
        inverse_amplitude = 1.0 / (total * (1.0 / count.astype(f32)) + 1e-06)
        for part in range(2):
            values = filtered[n, :, part * 128 : (part + 1) * 128] * inverse_amplitude
            own[group, part * tiles + n] = values.astype(bf16)
            windows = [values[w * C : (w + 1) * C] for w in range(W)]
            for d in (1, 2, 4):
                clear = lane // d % 2 == 0
                before = list(windows)
                for w in range(W):
                    if not w & d:
                        a, b = before[w], before[w | d]
                        windows[w] = jnp.where(clear, a, pltpu.roll(b, d * BINS, 1))
                        windows[w | d] = jnp.where(clear, pltpu.roll(a, 128 - d * BINS, 1), b)
            for m in range(per_tile):
                outgoing[home(n, m), :, part * 128 : (part + 1) * 128] = windows[m].astype(bf16)
        for m in range(per_tile):
            peer = home(n, m)

            @pl.when(peer != me)
            def _():
                exchange(lax.rem(peer - me + BLK, BLK)).start()

        for part in range(2):
            to_group(0, part * tiles + n, group, across).start()
            to_group(1, part * tiles + n, group, sibling).start()

    def stage(n):
        @pl.when(n < tiles)
        def _():
            transform(n)

        @pl.when((n >= 2) & (n < tiles + 2))
        def _():
            filter_tile(n - 2)

        @pl.when(n >= 3)
        def _():
            whiten_tile(n - 3)

    loop(0, tiles + 3, stage)
    mixed[me] = outgoing[me]

    wanted = jnp.where(iota((WIN * S, BLK * C), 1) == diagonal(sources[...].astype(f32), WIN * S).astype(i32), 1.0, 0.0).astype(bf16)
    span = 2 * W * BINS
    source = iota((span, 1), 0)
    window, one = lax.rem(source // BINS, W), lax.rem(source, BINS)
    pair, seat = one // PACK * 2 + lax.rem(one, 2), lax.rem(one // 2, 2)
    target = pair * 128 + lax.rem(window, 4) * 32 + seat * 16 + source // (W * BINS) * 8 + window // 4
    order = jnp.where(iota((span, WIN * span), 1) == target, 1.0, 0.0).astype(bf16)
    column = iota((1, 1024), 1)
    kind, part = lax.rem(column // 128, 2), lax.rem(column // 32, 2)
    origin = jnp.where(kind == part, 0, 128) + column // 256 * 32 + lax.rem(column, 32)
    sign = jnp.where(kind * part == 1, -1.0, 1.0)
    for b in range(PAIR):
        used = jnp.where(lax.rem(column // 64, 2) == b, origin, -1)
        spread_pair[b] = jnp.where(iota((256, 1024), 0) == used, sign, 0.0).astype(bf16)
    turn_group(group)
    loop(0, 2 * tiles, lambda t: to_group(1, t, sibling, sibling).wait_recv())
    turn_group(sibling)

    loop(1, BLK, lambda k: exchange(k).wait_recv())
    picked = mxu(wanted, mixed[...].reshape(BLK * C, 2 * W * BINS)).astype(bf16)
    chosen[...] = picked.reshape(WIN, S, 2 * W * BINS)

    def trade(k):
        peer = lax.rem(group + k, WIN)
        return win_copy(chosen.at[peer], regroup.at[group], win_send.at[k], win_recv.at[k], peer)

    loop(1, WIN, lambda k: trade(k).start())
    regroup[group] = chosen[group]

    def relay(t):
        to_group(0, t, across, across).wait_recv()
        to_group(2, t, across, sibling).start()

    loop(0, 2 * tiles, relay)
    turn_group(across)
    loop(1, WIN, lambda k: trade(k).wait_recv())
    arranged = mxu(regroup[0], order)
    for g in range(1, WIN):
        arranged += pltpu.roll(mxu(regroup[g], order), 2 * g, 1)
    for q in range(BINS // PACK):
        quads[q] = arranged[:, q * 256 : (q + 1) * 256].astype(bf16)

    def at(yy, zz, xx):
        return (lax.rem(yy + NY, NY) * NZ + lax.rem(zz, NZ)) * NX + lax.rem(xx + NX, NX)

    y_up, y_down, x_up, x_down, z_over = at(y + 1, z, x), at(y - 1, z, x), at(y, z, x + 1), at(y, z, x - 1), at(y, z + 1, x)

    first = ((y_up, y_down), (x_up, x_down))
    last = ((x_up, x_down), (y_up, y_down))
    per_half = BINS // PACK // 2

    def piece(block, half):
        return held.at[block, pl.ds(half * per_half, per_half)]

    def hop(block, half, slot, peer, src=None):
        src = piece(block, half) if src is None else src
        return chan_copy(src, piece(block, half), send.at[block, half, slot], recv.at[block, half], peer)

    def own_piece(half):
        return quads.at[pl.ds(half * per_half, per_half)]

    def arrived(block, half):
        hop(block, half, 0, z_over).wait_recv()

    def spread_last(block, half, src=None):
        hop(block, half, 3, last[half][0], src).start()
        hop(block, half, 4, last[half][1], src).start()

    def spread(block, half, src=None):
        hop(block, half, 1, first[half][0], src).start()
        hop(block, half, 2, first[half][1], src).start()
        spread_last(block, half, src)

    def walk(i):
        k = i // NZ
        k = jnp.where(k > 1, 5 - k, k)
        return lax.rem(y + k, NY), lax.rem(x + k, NX), lax.rem(i, NZ)

    for half in (0, 1):
        hop(me, half, 0, z_over, own_piece(half)).start()
    for half in (0, 1):
        spread(me, half, own_piece(half))
    for q in range(2 * per_half):
        held[me, q] = quads[q]

    for half in (0, 1):
        arrived(z_over, half)
        spread(z_over, half)

    loop(0, 2 * tiles, lambda t: to_group(2, t, diagonal_group, sibling).wait_recv())
    turn_group(diagonal_group)

    def widen(i):
        start = pl.multiple_of(i * 512, 512)
        real, imag = turned[pl.ds(start, 512), :], turned[pl.ds(F * 8 + start, 512), :]
        both = jnp.concatenate([real, imag], axis=1).reshape(16, 2, 16, 256)
        for b in range(PAIR):
            spread_rows = mxu(both[:, b].reshape(256, 256).astype(bf16), spread_pair[b])
            for p in range(4):
                upper = spread_rows[:, p * 256 : p * 256 + 128].reshape(32, 8, 128)
                lower = spread_rows[:, p * 256 + 128 : p * 256 + 256].reshape(32, 8, 128)
                tile = jnp.concatenate([upper, lower], axis=1).astype(bf16)
                wide[pl.ds(pl.multiple_of(i * 32, 32), 32), p * 32 + b * 16 : p * 32 + b * 16 + 16, :] = tile

    loop(0, F * 8 // 512, widen)

    def cross(block, half):
        for j in range(per_half):
            quad = place(block) * (2 * per_half) + half * per_half + j
            rows = pl.ds(pl.multiple_of(quad * S, S), S)
            for h in range(2):
                crossed[h, rows, :] = mxu(held[block, half * per_half + j, :, h * 128 : (h + 1) * 128], wide[quad * 2 + h])

    def near_block(half, step, zz):
        return at(y + step, zz, x) if half == 0 else at(y, zz, x + step)

    def far_block(half, step, along, zz):
        return at(along, zz, x + step) if half == 0 else at(y + step, zz, along)

    for zz in (z, z + 1):
        for half in (0, 1):
            for step in (-1, 1):
                block = near_block(half, step, zz)
                arrived(block, half)

                @pl.when(lax.rem(zz, NZ) == (0 if step == -1 else 1))
                def _():
                    hop(block, half, 1 if step == -1 else 2, first[half][0 if step == -1 else 1]).start()

                spread_last(block, half)

    for zz in (0, 1):
        for half in (0, 1):
            block = near_block(half, 2, zz)
            arrived(block, half)
            spread_last(block, half)

    ca, sa, cb, sb = row_cos[1:2, :], row_sin[1:2, :], step_cos[...], step_sin[...]
    near_cos[...] = jnp.concatenate([cb, ca * cb - sa * sb], axis=0).T
    near_sin[...] = jnp.concatenate([sb, sa * cb + ca * sb], axis=0).T
    lags = [128 // STEP * a - LAGS // 2 // STEP for a in range(LAGS // 128)]
    angles = [row_cos[abs(a) : abs(a) + 1, :] for a in lags]
    angles += [row_sin[abs(a) : abs(a) + 1, :] * (1.0 if a >= 0 else -1.0) for a in lags]
    far[...] = jnp.concatenate(angles + [jnp.zeros((128 - len(angles), F), f32)], axis=0).T
    for b in range(PAIR):
        for h in range(2):
            bins = pl.ds(2 * b + h, QUADS, stride=PACK)
            nc, ns, fc = near_cos[bins, :], near_sin[bins, :], far[bins, :]
            k = (h * 4 + b * 2) * QUADS
            for a in range(LAGS // 128):
                columns = slice(a * 128, (a + 1) * 128)
                ca, sa = fc[:, a : a + 1], fc[:, len(lags) + a : len(lags) + a + 1]
                inverse[k : k + QUADS, columns] = (ca * nc - sa * ns).astype(bf16)
                inverse[k + QUADS : k + 2 * QUADS, columns] = (-sa * nc - ca * ns).astype(bf16)
    inverse_copy = pltpu.make_async_copy(inverse, inverse_out, out_sem.at[0])
    inverse_copy.start()

    def far_pass(i):
        yy, xx, zz = walk(i)
        for half in (0, 1):
            for step in (-1, 1):
                block = far_block(half, step, yy if half == 0 else xx, zz)
                arrived(block, half)

                @pl.when(zz == (0 if step == -1 else 1))
                def _():
                    hop(block, half, 3 if step == -1 else 4, last[half][0 if step == -1 else 1]).start()

                cross(block, half)

    loop(0, NY * NZ, far_pass)

    def cross_near(i):
        yy, xx, zz = walk(i)
        cross(at(yy, zz, x), 0)
        cross(at(y, zz, xx), 1)

    loop(0, NY * NZ, cross_near)

    def far_last(i):
        yy, xx, zz = walk(i)
        for half in (0, 1):
            block = far_block(half, 2, yy if half == 0 else xx, zz)
            arrived(block, half)
            cross(block, half)

    loop(0, NY * NZ, far_last)

    def stacked_copy(first, count):
        where = pl.ds(pl.multiple_of(first, 8 * C), count)
        return pltpu.make_async_copy(stacked.at[where], stacked_out.at[where], out_sem.at[1])

    def turn_sources(i):
        for u in range(8):
            where = pl.ds(pl.multiple_of((i * 8 + u) * C, C), C)
            for h in range(2):
                flipped = crossed[h, pl.ds(i * 8 + u, QUADS, stride=S), :].T.astype(bf16)
                for k in range(4):
                    stacked[where, (h * 4 + k) * 128 : (h * 4 + k + 1) * 128] = flipped[k * 32 : (k + 1) * 32]
        stacked_copy(i * 8 * C, 8 * C).start()

    loop(0, S // 8, turn_sources)

    def finish_win(k):
        trade(k).wait_send()

    def finish_own(w):
        to_group(0, w, group, across).wait_send()
        to_group(1, w, group, sibling).wait_send()
        to_group(2, w, across, sibling).wait_send()

    def finish_halo(w):
        @pl.when(me < BLK - 1)
        def _():
            to_right(w).wait_send()

        @pl.when(me > 0)
        def _():
            to_left(w).wait_send()

    loop(1, WIN, finish_win)
    loop(0, 2 * tiles, finish_own)
    loop(1, BLK, lambda k: exchange(k).wait_send())
    loop(0, tiles, finish_halo)

    def sent(block, half, slot):
        hop(block, half, slot, z_over).wait_send()

    for half in (0, 1):
        sent(me, half, 0)
        for zz in (0, 1):
            for slot in (1, 2):
                sent(at(y, zz, x), half, slot)
        sent(near_block(half, -1, 0), half, 1)
        sent(near_block(half, 1, 1), half, 2)

    def sent_far(i):
        yy, xx, zz = walk(i)
        for half in (0, 1):
            block = at(yy, zz, x) if half == 0 else at(y, zz, xx)
            sent(block, half, 3)
            sent(block, half, 4)
            along = yy if half == 0 else xx

            @pl.when(zz == 0)
            def _():
                sent(far_block(half, -1, along, 0), half, 3)

            @pl.when(zz == 1)
            def _():
                sent(far_block(half, 1, along, 1), half, 4)

    loop(0, NY * NZ, sent_far)
    inverse_copy.wait()
    stacked_copy(0, S * C).wait()


def to_lags(scaling, stacked, inverse, out):
    out[...] = (mxu(stacked[...], inverse[...]) * scaling).reshape(out.shape)


def turn(bins, steps):
    phase = jnp.mod(bins * steps, L).astype(f32) * (2.0 * math.pi / L)
    return jnp.cos(phase), jnp.sin(phase)


def angle_parts():
    count = jnp.arange(40, dtype=i32)
    scale = jnp.where(count < 16, 8 * STEP, jnp.where(count < 24, STEP, jnp.where(count < 32, 8, 1)))
    steps = jnp.where(count < 16, count, count % 8) * scale
    return turn((K0 + jnp.arange(F, dtype=i32))[None, :], steps[:, None])


def per_device(traces, filter_taps, good_channels, source_index):
    vmem = pl.BlockSpec(memory_space=pltpu.VMEM)
    smem = pl.BlockSpec(memory_space=pltpu.SMEM)
    anywhere = pl.BlockSpec(memory_space=pl.ANY)
    dma = pltpu.SemaphoreType.DMA
    stacked, inverse = pl.pallas_call(
        whole,
        out_shape=(
            jax.ShapeDtypeStruct((S * C, 2 * F), bf16),
            jax.ShapeDtypeStruct((2 * F, LAGS), bf16),
        ),
        in_specs=[anywhere] + [vmem] * 5,
        out_specs=(anywhere, anywhere),
        scratch_shapes=[
            pltpu.VMEM((L // STEP, F), f32),
            pltpu.VMEM((L // STEP, F), f32),
            pltpu.VMEM((STEP, F), f32),
            pltpu.VMEM((STEP, F), f32),
            pltpu.VMEM((F, 128), f32),
            pltpu.VMEM((F, 128), f32),
            pltpu.VMEM((F, 128), f32),
            pltpu.VMEM((PAIR, 256, 1024), bf16),
            pltpu.VMEM((S * C, 2 * F), bf16),
            pltpu.VMEM((W * C, L), bf16),
            pltpu.VMEM((L, 256), bf16),
            pltpu.VMEM((F // 128, W, C, 256), f32),
            pltpu.VMEM((F // 128, W, HALO, 256), f32),
            pltpu.VMEM((F // 128, W, HALO, 256), f32),
            pltpu.VMEM((F // 128, W * C, 256), f32),
            pltpu.VMEM((3 * W * C, F + 256), bf16),
            pltpu.VMEM((BLK, C, 2 * W * BINS), bf16),
            pltpu.VMEM((BLK, C, 2 * W * BINS), bf16),
            pltpu.VMEM((WIN, S, 2 * W * BINS), bf16),
            pltpu.VMEM((WIN, S, 2 * W * BINS), bf16),
            pltpu.VMEM((WIN, 2 * F // 128, W * C, 128), bf16),
            pltpu.VMEM((BINS // PACK, S, 256), bf16),
            pltpu.VMEM((BLK, BINS // PACK, S, 256), bf16),
            pltpu.VMEM((F * 16, 128), f32),
            pltpu.VMEM((QUADS * 2, 128, 128), bf16),
            pltpu.VMEM((2, QUADS * S, 128), f32),
            pltpu.VMEM((2 * F, LAGS), bf16),
            dma((2, F // 128)), dma((2, F // 128)), dma((BLK,)), dma((BLK,)),
            dma((3, 2 * F // 128)), dma((3, 2 * F // 128)), dma((WIN,)), dma((WIN,)),
            dma((BLK, 2, 5)), dma((BLK, 2)), dma((3,)),
        ],
        compiler_params=pltpu.CompilerParams(
            collective_id=0, has_side_effects=True, vmem_limit_bytes=LIMIT << 20
        ),
        name="whole",
    )(
        traces.reshape(W * C, L), good_channels.astype(i32)[None, :], filter_taps[None, :],
        source_index.astype(i32)[None, :], *angle_parts(),
    )

    scaling = 1.0 / math.sqrt(F * W * WIN)
    return pl.pallas_call(
        functools.partial(to_lags, scaling),
        grid=(S // AT_ONCE,),
        out_shape=jax.ShapeDtypeStruct((S, C, LAGS), f32),
        in_specs=[
            pl.BlockSpec((AT_ONCE * C, 2 * F), lambda i: (i, 0)),
            pl.BlockSpec((2 * F, LAGS), lambda i: (0, 0), pipeline_mode=pl.Buffered(1)),
        ],
        out_specs=pl.BlockSpec((AT_ONCE, C, LAGS), lambda i: (i, 0, 0)),
        compiler_params=pltpu.CompilerParams(vmem_limit_bytes=62 << 20),
        name="to_lags",
    )(stacked, inverse)


def solution(mesh):
    placed = (P("win", "chan", None), P(), P("chan"), P())
    return jax.shard_map(
        per_device, mesh=mesh, in_specs=placed, out_specs=P("win", "chan", None), check_vma=False
    )
```

```python
import functools
import math

import jax
import jax.numpy as jnp
from jax import lax
from jax.experimental import pallas as pl
from jax.experimental.pallas import tpu as pltpu
from jax.sharding import PartitionSpec as P

L = 7680
F = 512
LAGS = 2048
HALO = 16
SMOOTH = 64
K0 = 31

WIN = 4
BLK = 32
NX = 4
NZ = 2
NY = 4
W = 8
C = 32
S = 64
BINS = F // BLK
QUADS = F // 4
PACK = 4
PAIR = 2
LIMIT = 54
AT_ONCE = 16
STEP = 64
DEEP = 2 * W * WIN
MESH = pl.DeviceIdType.MESH
f32, bf16, i32 = jnp.float32, jnp.bfloat16, jnp.int32


def iota(shape, dim):
    return lax.broadcasted_iota(i32, shape, dim)


def mxu(a, b):
    return jnp.dot(a, b, preferred_element_type=f32)


def loop(start, stop, body):
    def step(i, carry):
        body(i)
        return carry

    lax.fori_loop(start, stop, step, 0)


def thirds(x):
    high = x.astype(bf16)
    rest = x - high.astype(f32)
    middle = rest.astype(bf16)
    low = (rest - middle.astype(f32)).astype(bf16)
    return high, middle, low


def chan_copy(src, dst, send, recv, peer):
    return pltpu.make_async_remote_copy(
        src_ref=src, dst_ref=dst, send_sem=send, recv_sem=recv,
        device_id=(lax.axis_index("win"), peer), device_id_type=MESH,
    )


def win_copy(src, dst, send, recv, peer):
    return pltpu.make_async_remote_copy(
        src_ref=src, dst_ref=dst, send_sem=send, recv_sem=recv,
        device_id=(peer, lax.axis_index("chan")), device_id_type=MESH,
    )


def diagonal(row, count):
    return jnp.sum(jnp.where(iota((count, count), 0) == iota((count, count), 1), row, 0.0), axis=1, keepdims=True)


def whole(
    traces, good, taps, sources, cosines, sines, stacked_out, inverse_out,
    row_cos, row_sin, step_cos, step_sin, near_cos, near_sin, far, spread_pair, stacked, rows, table, spec, low, high, filtered, magnitudes, outgoing, mixed, chosen, regroup, own, quads, held, turned, wide,
    crossed, inverse,
    halo_send, halo_recv, all_send, all_recv, own_send, own_recv, win_send, win_recv, send, recv, out_sem,
):
    me = lax.axis_index("chan")
    group = lax.axis_index("win")
    y, z, x = me // (NZ * NX), lax.rem(me // NX, NZ), lax.rem(me, NX)
    layer, core = group // 2, lax.rem(group, 2)
    sibling, across, diagonal_group = layer * 2 + 1 - core, (1 - layer) * 2 + core, (1 - layer) * 2 + 1 - core

    rows_in = pltpu.make_async_copy(traces, rows, out_sem.at[2])
    rows_in.start()
    barrier = pltpu.get_barrier_semaphore()

    def greet_chan(k):
        pl.semaphore_signal(barrier, inc=1, device_id=(group, lax.rem(me + k, BLK)), device_id_type=MESH)

    def greet_win(k):
        pl.semaphore_signal(barrier, inc=1, device_id=(lax.rem(group + k, WIN), me), device_id_type=MESH)

    loop(1, BLK, greet_chan)
    loop(1, WIN, greet_win)

    offset = iota((C, C + 2 * HALO), 1) - iota((C, C + 2 * HALO), 0)
    weights = taps[...].astype(f32)
    band = jnp.where(offset == HALO, 1.0, 0.0)
    for o in range(HALO):
        band = jnp.where(offset == o, -weights[:, o : o + 1], band)
        band = jnp.where(offset == HALO + 1 + o, -weights[:, HALO + o : HALO + o + 1], band)
    band = jnp.concatenate([band, band, band], axis=1).astype(bf16)
    keep = diagonal(good[...].astype(f32), C)
    beside = jnp.where(jnp.abs(iota((384, 128), 0) - 128 - iota((384, 128), 1)) <= SMOOTH, 1.0, 0.0).astype(bf16)
    magnitudes[:, 0:128] = jnp.zeros((3 * W * C, 128), bf16)
    magnitudes[:, 640:768] = jnp.zeros((3 * W * C, 128), bf16)

    @pl.when(me == 0)
    def _():
        low[...] = jnp.zeros_like(low)

    @pl.when(me == BLK - 1)
    def _():
        high[...] = jnp.zeros_like(high)

    def sums(a, b):
        ca, sa, cb, sb = cosines[a, :], sines[a, :], cosines[b, :], sines[b, :]
        return ca * cb - sa * sb, sa * cb + ca * sb

    for i in range(L // STEP // 8):
        row_cos[i * 8 : (i + 1) * 8, :], row_sin[i * 8 : (i + 1) * 8, :] = sums(slice(i, i + 1), slice(16, 24))
    for i in range(STEP // 8):
        step_cos[i * 8 : (i + 1) * 8, :], step_sin[i * 8 : (i + 1) * 8, :] = sums(slice(24 + i, 25 + i), slice(32, 40))

    tiles = F // 128
    per_tile = 128 // BINS
    right, left = lax.rem(me + 1, BLK), lax.rem(me + BLK - 1, BLK)

    def to_right(n):
        return chan_copy(spec.at[n, :, pl.ds(C - HALO, HALO)], low.at[n], halo_send.at[0, n], halo_recv.at[0, n], right)

    def to_left(n):
        return chan_copy(spec.at[n, :, pl.ds(0, HALO)], high.at[n], halo_send.at[1, n], halo_recv.at[1, n], left)

    def tile_of(n):
        return pl.ds(pl.multiple_of(n * 128, 128), 128)

    def transform(n):
        columns = tile_of(n)
        cb, sb = step_cos[:, columns], step_sin[:, columns]

        def table_rows(i):
            eight = pl.ds(pl.multiple_of(i * 8, 8), 8)
            cas, sas = row_cos[eight, columns], row_sin[eight, columns]
            for u in range(8):
                ca, sa = cas[u : u + 1], sas[u : u + 1]
                at_rows = pl.ds(pl.multiple_of((i * 8 + u) * STEP, STEP), STEP)
                table[at_rows, 0:128] = (ca * cb - sa * sb).astype(bf16)
                table[at_rows, 128:256] = (-sa * cb - ca * sb).astype(bf16)

        loop(0, L // STEP // 8, table_rows)

        @pl.when(n == 0)
        def _():
            rows_in.wait()

        spec[n] = mxu(rows[...], table[...]).reshape(W, C, 256) * keep

        @pl.when(n == 0)
        def _():
            pl.semaphore_wait(barrier, BLK + WIN - 2)

        @pl.when(me < BLK - 1)
        def _():
            to_right(n).start()

        @pl.when(me > 0)
        def _():
            to_left(n).start()

    def filter_tile(n):
        @pl.when(me > 0)
        def _():
            to_right(n).wait_recv()

        @pl.when(me < BLK - 1)
        def _():
            to_left(n).wait_recv()

        for w in range(W):
            padded = jnp.concatenate([low[n, w], spec[n, w], high[n, w]], axis=0)
            out = mxu(band, jnp.concatenate(thirds(padded), axis=0)) * keep
            filtered[n, w * C : (w + 1) * C, :] = out
            real, imag = out[:, :128], out[:, 128:]
            for k, part in enumerate(thirds(jnp.sqrt(real * real + imag * imag))):
                magnitudes[(k * W + w) * C : (k * W + w + 1) * C, tile_of(n + 1)] = part

    lane = iota((C, 128), 1) // BINS

    def exchange(k):
        peer = lax.rem(me + k, BLK)
        return chan_copy(outgoing.at[peer], mixed.at[me], all_send.at[k], all_recv.at[k], peer)

    def to_group(hop, tile, whose, peer):
        return win_copy(own.at[whose, tile], own.at[whose, tile], own_send.at[hop, tile], own_recv.at[hop, tile], peer)

    def turn_tile(whose, part, tile):
        for half in range(2):
            block = own[whose, part * tiles + tile, half * 128 : (half + 1) * 128, :]
            start = part * F * 8 + tile * 128 * 8 + whose * 2 + half
            turned[pl.ds(start, 128, stride=8), :] = block.astype(f32).T

    def turn_group(whose):
        def both(tile):
            turn_tile(whose, 0, tile)
            turn_tile(whose, 1, tile)

        loop(0, tiles, both)

    def home(n, m):
        return (m // NZ) * NZ * NX + (m % NZ) * NX + lax.rem(n + m // NZ, NX)

    def place(block):
        yy, zz, xx = block // (NZ * NX), lax.rem(block // NX, NZ), lax.rem(block, NX)
        return lax.rem(xx - yy + NX, NX) * per_tile + yy * NZ + zz

    def whiten_tile(n):
        sums = mxu(magnitudes[:, pl.ds(pl.multiple_of(n * 128, 128), 384)], beside)
        bins = iota((1, 128), 1) + n * 128
        count = 1 + jnp.minimum(bins, SMOOTH) + jnp.minimum(F - 1 - bins, SMOOTH)
        total = sums[: W * C] + sums[W * C : 2 * W * C] + sums[2 * W * C :]
        inverse_amplitude = 1.0 / (total * (1.0 / count.astype(f32)) + 1e-06)
        for part in range(2):
            values = filtered[n, :, part * 128 : (part + 1) * 128] * inverse_amplitude
            own[group, part * tiles + n] = values.astype(bf16)
            windows = [values[w * C : (w + 1) * C] for w in range(W)]
            for d in (1, 2, 4):
                clear = lane // d % 2 == 0
                before = list(windows)
                for w in range(W):
                    if not w & d:
                        a, b = before[w], before[w | d]
                        windows[w] = jnp.where(clear, a, pltpu.roll(b, d * BINS, 1))
                        windows[w | d] = jnp.where(clear, pltpu.roll(a, 128 - d * BINS, 1), b)
            for m in range(per_tile):
                outgoing[home(n, m), :, part * 128 : (part + 1) * 128] = windows[m].astype(bf16)
        for m in range(per_tile):
            peer = home(n, m)

            @pl.when(peer != me)
            def _():
                exchange(lax.rem(peer - me + BLK, BLK)).start()

        for part in range(2):
            to_group(0, part * tiles + n, group, across).start()
            to_group(1, part * tiles + n, group, sibling).start()

    def stage(n):
        @pl.when(n < tiles)
        def _():
            transform(n)

        @pl.when((n >= 2) & (n < tiles + 2))
        def _():
            filter_tile(n - 2)

        @pl.when(n >= 3)
        def _():
            whiten_tile(n - 3)

    loop(0, tiles + 3, stage)
    mixed[me] = outgoing[me]

    wanted = jnp.where(iota((WIN * S, BLK * C), 1) == diagonal(sources[...].astype(f32), WIN * S).astype(i32), 1.0, 0.0).astype(bf16)
    span = 2 * W * BINS
    source = iota((span, 1), 0)
    window, one = lax.rem(source // BINS, W), lax.rem(source, BINS)
    pair, seat = one // PACK * 2 + lax.rem(one, 2), lax.rem(one // 2, 2)
    target = pair * 128 + lax.rem(window, 4) * 32 + seat * 16 + source // (W * BINS) * 8 + window // 4
    order = jnp.where(iota((span, WIN * span), 1) == target, 1.0, 0.0).astype(bf16)
    column = iota((1, 1024), 1)
    kind, part = lax.rem(column // 128, 2), lax.rem(column // 32, 2)
    origin = jnp.where(kind == part, 0, 128) + column // 256 * 32 + lax.rem(column, 32)
    sign = jnp.where(kind * part == 1, -1.0, 1.0)
    for b in range(PAIR):
        used = jnp.where(lax.rem(column // 64, 2) == b, origin, -1)
        spread_pair[b] = jnp.where(iota((256, 1024), 0) == used, sign, 0.0).astype(bf16)
    turn_group(group)
    loop(0, 2 * tiles, lambda t: to_group(1, t, sibling, sibling).wait_recv())
    turn_group(sibling)

    loop(1, BLK, lambda k: exchange(k).wait_recv())
    picked = mxu(wanted, mixed[...].reshape(BLK * C, 2 * W * BINS)).astype(bf16)
    chosen[...] = picked.reshape(WIN, S, 2 * W * BINS)

    def trade(k):
        peer = lax.rem(group + k, WIN)
        return win_copy(chosen.at[peer], regroup.at[group], win_send.at[k], win_recv.at[k], peer)

    loop(1, WIN, lambda k: trade(k).start())
    regroup[group] = chosen[group]

    def relay(t):
        to_group(0, t, across, across).wait_recv()
        to_group(2, t, across, sibling).start()

    loop(0, 2 * tiles, relay)
    turn_group(across)
    loop(1, WIN, lambda k: trade(k).wait_recv())
    arranged = mxu(regroup[0], order)
    for g in range(1, WIN):
        arranged += pltpu.roll(mxu(regroup[g], order), 2 * g, 1)
    for q in range(BINS // PACK):
        quads[q] = arranged[:, q * 256 : (q + 1) * 256].astype(bf16)

    def at(yy, zz, xx):
        return (lax.rem(yy + NY, NY) * NZ + lax.rem(zz, NZ)) * NX + lax.rem(xx + NX, NX)

    y_up, y_down, x_up, x_down, z_over = at(y + 1, z, x), at(y - 1, z, x), at(y, z, x + 1), at(y, z, x - 1), at(y, z + 1, x)

    first = ((y_up, y_down), (x_up, x_down))
    last = ((x_up, x_down), (y_up, y_down))
    per_half = BINS // PACK // 2

    def piece(block, half):
        return held.at[block, pl.ds(half * per_half, per_half)]

    def hop(block, half, slot, peer, src=None):
        src = piece(block, half) if src is None else src
        return chan_copy(src, piece(block, half), send.at[block, half, slot], recv.at[block, half], peer)

    def own_piece(half):
        return quads.at[pl.ds(half * per_half, per_half)]

    def arrived(block, half):
        hop(block, half, 0, z_over).wait_recv()

    def spread_last(block, half, src=None):
        hop(block, half, 3, last[half][0], src).start()
        hop(block, half, 4, last[half][1], src).start()

    def spread(block, half, src=None):
        hop(block, half, 1, first[half][0], src).start()
        hop(block, half, 2, first[half][1], src).start()
        spread_last(block, half, src)

    def walk(i):
        k = i // NZ
        k = jnp.where(k > 1, 5 - k, k)
        return lax.rem(y + k, NY), lax.rem(x + k, NX), lax.rem(i, NZ)

    for half in (0, 1):
        hop(me, half, 0, z_over, own_piece(half)).start()
    for half in (0, 1):
        spread(me, half, own_piece(half))
    for q in range(2 * per_half):
        held[me, q] = quads[q]

    ca, sa, cb, sb = row_cos[1:2, :], row_sin[1:2, :], step_cos[...], step_sin[...]
    near_cos[...] = jnp.concatenate([cb, ca * cb - sa * sb], axis=0).T
    near_sin[...] = jnp.concatenate([sb, sa * cb + ca * sb], axis=0).T
    lags = [128 // STEP * a - LAGS // 2 // STEP for a in range(LAGS // 128)]
    angles = [row_cos[abs(a) : abs(a) + 1, :] for a in lags]
    angles += [row_sin[abs(a) : abs(a) + 1, :] * (1.0 if a >= 0 else -1.0) for a in lags]
    far[...] = jnp.concatenate(angles + [jnp.zeros((128 - len(angles), F), f32)], axis=0).T
    for b in range(PAIR):
        for h in range(2):
            bins = pl.ds(2 * b + h, QUADS, stride=PACK)
            nc, ns, fc = near_cos[bins, :], near_sin[bins, :], far[bins, :]
            k = (h * 4 + b * 2) * QUADS
            for a in range(LAGS // 128):
                columns = slice(a * 128, (a + 1) * 128)
                ca, sa = fc[:, a : a + 1], fc[:, len(lags) + a : len(lags) + a + 1]
                inverse[k : k + QUADS, columns] = (ca * nc - sa * ns).astype(bf16)
                inverse[k + QUADS : k + 2 * QUADS, columns] = (-sa * nc - ca * ns).astype(bf16)
    inverse_copy = pltpu.make_async_copy(inverse, inverse_out, out_sem.at[0])
    inverse_copy.start()

    for half in (0, 1):
        arrived(z_over, half)
        spread(z_over, half)

    loop(0, 2 * tiles, lambda t: to_group(2, t, diagonal_group, sibling).wait_recv())
    turn_group(diagonal_group)

    def widen(i):
        start = pl.multiple_of(i * 512, 512)
        real, imag = turned[pl.ds(start, 512), :], turned[pl.ds(F * 8 + start, 512), :]
        both = jnp.concatenate([real, imag], axis=1).reshape(16, 2, 16, 256)
        for b in range(PAIR):
            spread_rows = mxu(both[:, b].reshape(256, 256).astype(bf16), spread_pair[b])
            for p in range(4):
                upper = spread_rows[:, p * 256 : p * 256 + 128].reshape(32, 8, 128)
                lower = spread_rows[:, p * 256 + 128 : p * 256 + 256].reshape(32, 8, 128)
                tile = jnp.concatenate([upper, lower], axis=1).astype(bf16)
                wide[pl.ds(pl.multiple_of(i * 32, 32), 32), p * 32 + b * 16 : p * 32 + b * 16 + 16, :] = tile

    loop(0, F * 8 // 512, widen)

    def cross(block, half):
        for j in range(per_half):
            quad = place(block) * (2 * per_half) + half * per_half + j
            rows = pl.ds(pl.multiple_of(quad * S, S), S)
            for h in range(2):
                crossed[h, rows, :] = mxu(held[block, half * per_half + j, :, h * 128 : (h + 1) * 128], wide[quad * 2 + h])

    def near_block(half, step, zz):
        return at(y + step, zz, x) if half == 0 else at(y, zz, x + step)

    def far_block(half, step, along, zz):
        return at(along, zz, x + step) if half == 0 else at(y + step, zz, along)

    for zz in (z, z + 1):
        for half in (0, 1):
            for step in (-1, 1):
                block = near_block(half, step, zz)
                arrived(block, half)

                @pl.when(lax.rem(zz, NZ) == (0 if step == -1 else 1))
                def _():
                    hop(block, half, 1 if step == -1 else 2, first[half][0 if step == -1 else 1]).start()

                spread_last(block, half)

    for zz in (0, 1):
        for half in (0, 1):
            block = near_block(half, 2, zz)
            arrived(block, half)
            spread_last(block, half)

    def far_pass(i):
        yy, xx, zz = walk(i)
        for half in (0, 1):
            for step in (-1, 1):
                block = far_block(half, step, yy if half == 0 else xx, zz)
                arrived(block, half)

                @pl.when(zz == (0 if step == -1 else 1))
                def _():
                    hop(block, half, 3 if step == -1 else 4, last[half][0 if step == -1 else 1]).start()

                cross(block, half)

    loop(0, NY * NZ, far_pass)

    def cross_near(i):
        yy, xx, zz = walk(i)
        cross(at(yy, zz, x), 0)
        cross(at(y, zz, xx), 1)

    loop(0, NY * NZ, cross_near)

    def far_last(i):
        yy, xx, zz = walk(i)
        for half in (0, 1):
            block = far_block(half, 2, yy if half == 0 else xx, zz)
            arrived(block, half)
            cross(block, half)

    loop(0, NY * NZ, far_last)

    def stacked_copy(first, count):
        where = pl.ds(pl.multiple_of(first, 8 * C), count)
        return pltpu.make_async_copy(stacked.at[where], stacked_out.at[where], out_sem.at[1])

    def turn_sources(i):
        for u in range(8):
            where = pl.ds(pl.multiple_of((i * 8 + u) * C, C), C)
            for h in range(2):
                flipped = crossed[h, pl.ds(i * 8 + u, QUADS, stride=S), :].T.astype(bf16)
                for k in range(4):
                    stacked[where, (h * 4 + k) * 128 : (h * 4 + k + 1) * 128] = flipped[k * 32 : (k + 1) * 32]
        stacked_copy(i * 8 * C, 8 * C).start()

    loop(0, S // 8, turn_sources)

    def finish_win(k):
        trade(k).wait_send()

    def finish_own(w):
        to_group(0, w, group, across).wait_send()
        to_group(1, w, group, sibling).wait_send()
        to_group(2, w, across, sibling).wait_send()

    def finish_halo(w):
        @pl.when(me < BLK - 1)
        def _():
            to_right(w).wait_send()

        @pl.when(me > 0)
        def _():
            to_left(w).wait_send()

    loop(1, WIN, finish_win)
    loop(0, 2 * tiles, finish_own)
    loop(1, BLK, lambda k: exchange(k).wait_send())
    loop(0, tiles, finish_halo)

    def sent(block, half, slot):
        hop(block, half, slot, z_over).wait_send()

    for half in (0, 1):
        sent(me, half, 0)
        for zz in (0, 1):
            for slot in (1, 2):
                sent(at(y, zz, x), half, slot)
        sent(near_block(half, -1, 0), half, 1)
        sent(near_block(half, 1, 1), half, 2)

    def sent_far(i):
        yy, xx, zz = walk(i)
        for half in (0, 1):
            block = at(yy, zz, x) if half == 0 else at(y, zz, xx)
            sent(block, half, 3)
            sent(block, half, 4)
            along = yy if half == 0 else xx

            @pl.when(zz == 0)
            def _():
                sent(far_block(half, -1, along, 0), half, 3)

            @pl.when(zz == 1)
            def _():
                sent(far_block(half, 1, along, 1), half, 4)

    loop(0, NY * NZ, sent_far)
    inverse_copy.wait()
    stacked_copy(0, S * C).wait()


def to_lags(scaling, stacked, inverse, out):
    out[...] = (mxu(stacked[...], inverse[...]) * scaling).reshape(out.shape)


def turn(bins, steps):
    phase = jnp.mod(bins * steps, L).astype(f32) * (2.0 * math.pi / L)
    return jnp.cos(phase), jnp.sin(phase)


def angle_parts():
    count = jnp.arange(40, dtype=i32)
    scale = jnp.where(count < 16, 8 * STEP, jnp.where(count < 24, STEP, jnp.where(count < 32, 8, 1)))
    steps = jnp.where(count < 16, count, count % 8) * scale
    return turn((K0 + jnp.arange(F, dtype=i32))[None, :], steps[:, None])


def per_device(traces, filter_taps, good_channels, source_index):
    vmem = pl.BlockSpec(memory_space=pltpu.VMEM)
    smem = pl.BlockSpec(memory_space=pltpu.SMEM)
    anywhere = pl.BlockSpec(memory_space=pl.ANY)
    dma = pltpu.SemaphoreType.DMA
    stacked, inverse = pl.pallas_call(
        whole,
        out_shape=(
            jax.ShapeDtypeStruct((S * C, 2 * F), bf16),
            jax.ShapeDtypeStruct((2 * F, LAGS), bf16),
        ),
        in_specs=[anywhere] + [vmem] * 5,
        out_specs=(anywhere, anywhere),
        scratch_shapes=[
            pltpu.VMEM((L // STEP, F), f32),
            pltpu.VMEM((L // STEP, F), f32),
            pltpu.VMEM((STEP, F), f32),
            pltpu.VMEM((STEP, F), f32),
            pltpu.VMEM((F, 128), f32),
            pltpu.VMEM((F, 128), f32),
            pltpu.VMEM((F, 128), f32),
            pltpu.VMEM((PAIR, 256, 1024), bf16),
            pltpu.VMEM((S * C, 2 * F), bf16),
            pltpu.VMEM((W * C, L), bf16),
            pltpu.VMEM((L, 256), bf16),
            pltpu.VMEM((F // 128, W, C, 256), f32),
            pltpu.VMEM((F // 128, W, HALO, 256), f32),
            pltpu.VMEM((F // 128, W, HALO, 256), f32),
            pltpu.VMEM((F // 128, W * C, 256), f32),
            pltpu.VMEM((3 * W * C, F + 256), bf16),
            pltpu.VMEM((BLK, C, 2 * W * BINS), bf16),
            pltpu.VMEM((BLK, C, 2 * W * BINS), bf16),
            pltpu.VMEM((WIN, S, 2 * W * BINS), bf16),
            pltpu.VMEM((WIN, S, 2 * W * BINS), bf16),
            pltpu.VMEM((WIN, 2 * F // 128, W * C, 128), bf16),
            pltpu.VMEM((BINS // PACK, S, 256), bf16),
            pltpu.VMEM((BLK, BINS // PACK, S, 256), bf16),
            pltpu.VMEM((F * 16, 128), f32),
            pltpu.VMEM((QUADS * 2, 128, 128), bf16),
            pltpu.VMEM((2, QUADS * S, 128), f32),
            pltpu.VMEM((2 * F, LAGS), bf16),
            dma((2, F // 128)), dma((2, F // 128)), dma((BLK,)), dma((BLK,)),
            dma((3, 2 * F // 128)), dma((3, 2 * F // 128)), dma((WIN,)), dma((WIN,)),
            dma((BLK, 2, 5)), dma((BLK, 2)), dma((3,)),
        ],
        compiler_params=pltpu.CompilerParams(
            collective_id=0, has_side_effects=True, vmem_limit_bytes=LIMIT << 20
        ),
        name="whole",
    )(
        traces.reshape(W * C, L), good_channels.astype(i32)[None, :], filter_taps[None, :],
        source_index.astype(i32)[None, :], *angle_parts(),
    )

    scaling = 1.0 / math.sqrt(F * W * WIN)
    return pl.pallas_call(
        functools.partial(to_lags, scaling),
        grid=(S // AT_ONCE,),
        out_shape=jax.ShapeDtypeStruct((S, C, LAGS), f32),
        in_specs=[
            pl.BlockSpec((AT_ONCE * C, 2 * F), lambda i: (i, 0)),
            pl.BlockSpec((2 * F, LAGS), lambda i: (0, 0), pipeline_mode=pl.Buffered(1)),
        ],
        out_specs=pl.BlockSpec((AT_ONCE, C, LAGS), lambda i: (i, 0, 0)),
        compiler_params=pltpu.CompilerParams(vmem_limit_bytes=62 << 20),
        name="to_lags",
    )(stacked, inverse)


def solution(mesh):
    placed = (P("win", "chan", None), P(), P("chan"), P())
    return jax.shard_map(
        per_device, mesh=mesh, in_specs=placed, out_specs=P("win", "chan", None), check_vma=False
    )
```
